32 devices in a mesh: dp: 16 (over z, y, x), tensor: 2 (over core).
Axes of the slice: x: 2, y: 2, z: 4, core: 2. Of those that a mesh axis runs over, the one named last changes fastest.
Arguments:
- tokens: bfloat16 [32768, 768], P(('dp', 'tensor')), may hold values from -6 to 6
- prefix: int32 [16], P('dp'), may hold values from 204 to 1024
- qkv_latent: float32 [3, 768, 768], P(None, None, ('tensor', 'dp')), may hold values from -0.4375 to 0.4375
- out_latent: float32 [768, 768], P(('tensor', 'dp')), may hold values from -0.875 to 0.875
- up_latent: float32 [768, 3072], P(None, ('tensor', 'dp')), may hold values from -0.21875 to 0.21875
- down_latent: float32 [3072, 768], P(('tensor', 'dp')), may hold values from -0.109375 to 0.109375
- head_bias: float32 [2, 768], P(None, ('dp', 'tensor')), may hold values from -3 to 3
- up_bias: float32 [3072], P(('dp', 'tensor')), may hold values from -3 to 3
- row_params: float32 [6, 768], P(None, ('dp', 'tensor'))
- teacher_qkv: bfloat16 [3, 768, 768], P(None, None, ('tensor', 'dp')), may hold values from -0.3125 to 0.3125
- teacher_out: bfloat16 [768, 768], P(('tensor', 'dp')), may hold values from -0.875 to 0.875
- teacher_up: bfloat16 [768, 3072], P(None, ('tensor', 'dp')), may hold values from -0.21875 to 0.21875
- teacher_down: bfloat16 [3072, 768], P(('tensor', 'dp')), may hold values from -0.109375 to 0.109375
- teacher_head_bias: float32 [2, 768], P(None, ('dp', 'tensor')), may hold values from -3 to 3
- teacher_up_bias: float32 [3072], P(('dp', 'tensor')), may hold values from -3 to 3
- teacher_rows: float32 [6, 768], P(None, ('dp', 'tensor'))
Outputs:
- out: bfloat16 [32768, 768], P(('dp', 'tensor'))
- token_grad: float32 [32768, 768], P(('dp', 'tensor'))
- qkv_grad: float32 [3, 768, 768], P(None, None, ('tensor', 'dp'))
- out_grad: float32 [768, 768], P(('tensor', 'dp'))
- up_grad: float32 [768, 3072], P(None, ('tensor', 'dp'))
- down_grad: float32 [3072, 768], P(('tensor', 'dp'))
- head_bias_grad: float32 [2, 768], P(None, ('dp', 'tensor'))
- up_bias_grad: float32 [3072], P(('dp', 'tensor'))
- row_grad: float32 [6, 768], P(None, ('dp', 'tensor'))
The draws below stay inside these ranges and needn't reach their ends.
All inputs are finite; a program needn't handle non-finite values.
Results may differ from the reference program's by a relative error of at most 0.014.
The reference program's roundings to bfloat16 on the way count: a program that leaves them out, or rounds other values in their place, can miss the bound.
Values may be sent and summed in bfloat16 or wider, within the bound.
No kernel may reach another device: no remote copies, remote signals or barrier semaphores. Data moves between devices by JAX's collectives and lax.ppermute only.
A program may use at most 384 MiB of HBM per device.

```python
import math
import jax
import jax.numpy as jnp
from jax import lax

D = 768
HEADS = 12
FF = 3072
HEAD = 64
LEN = 2048
SEQS = 16
TOKENS = 32768


def norm_table(key):
    noise = jax.random.normal(jax.random.fold_in(key, 7), (6, D), jnp.float32) * 0.5
    gains = jax.random.uniform(jax.random.fold_in(key, 11), (6, D), jnp.float32, 0.5, 1.5)
    indices = jnp.arange(6)
    is_gain = (indices % 2 == 0) & (indices >= 2)
    return jnp.where(is_gain[:, None], gains, noise)


def draw_row_params(key, part):
    return norm_table(jax.random.fold_in(key, 1))


def draw_teacher_rows(key, part):
    return norm_table(jax.random.fold_in(key, 2))


def draw_prefix(key, part):
    lengths = jax.random.randint(jax.random.fold_in(key, 3), (SEQS,), LEN // 10, LEN // 2 + 1)
    lengths = lengths.at[0].set(LEN // 2)
    return lengths.at[SEQS - 1].set(LEN // 10)


def shard_levels(stream_key, extent, cuts, least, largest):
    factor_of = 1.0
    for dim, shards_of in cuts:
        steps = jax.random.uniform(jax.random.fold_in(jax.random.fold_in(stream_key, 6), dim), (shards_of,), jnp.float32, least / len(cuts), largest / len(cuts))
        factor_of = factor_of * jnp.repeat(jnp.exp(steps), extent[dim] // shards_of).reshape((-1,) + (1,) * (len(extent) - 1 - dim))
    return factor_of


def gaussian(own_key, shape, width, reach, split=(), kind=jnp.bfloat16):
    drawn = width * jax.random.normal(own_key, shape, jnp.float32)
    if split:
        drawn = drawn * shard_levels(own_key, shape, split, -0.22, 0.18)
    return jnp.clip(drawn, -reach, reach).astype(kind)


def setup_inputs(seed: int = 0) -> dict:
    splits = jax.random.split(jax.random.key(seed), 17)
    return {
        "tokens": gaussian(splits[0], (TOKENS, D), 1.0, 6.0, ((0, 32),)),
        "prefix": draw_prefix(jax.random.fold_in(splits[16], 71), 0),
        "qkv_latent": gaussian(splits[2], (3, D, D), (D // 4) ** -0.5, 0.4375, ((2, 32),), jnp.float32),
        "out_latent": gaussian(splits[3], (D, D), (D // 16) ** -0.5, 0.875, ((0, 32),), jnp.float32),
        "up_latent": gaussian(splits[4], (D, FF), D ** -0.5, 0.21875, ((1, 32),), jnp.float32),
        "down_latent": gaussian(splits[5], (FF, D), FF ** -0.5, 0.109375, ((0, 32),), jnp.float32),
        "head_bias": gaussian(splits[6], (2, D), 0.5, 3.0, ((1, 32),), jnp.float32),
        "up_bias": gaussian(splits[7], (FF,), 0.5, 3.0, ((0, 32),), jnp.float32),
        "row_params": draw_row_params(jax.random.fold_in(splits[16], 71), 0),
        "teacher_qkv": gaussian(splits[9], (3, D, D), (D // 2) ** -0.5, 0.3125, ((2, 32),)),
        "teacher_out": gaussian(splits[10], (D, D), (D // 16) ** -0.5, 0.875, ((0, 32),)),
        "teacher_up": gaussian(splits[11], (D, FF), D ** -0.5, 0.21875, ((1, 32),)),
        "teacher_down": gaussian(splits[12], (FF, D), FF ** -0.5, 0.109375, ((0, 32),)),
        "teacher_head_bias": gaussian(splits[13], (2, D), 0.5, 3.0, ((1, 32),), jnp.float32),
        "teacher_up_bias": gaussian(splits[14], (FF,), 0.5, 3.0, ((0, 32),), jnp.float32),
        "teacher_rows": draw_teacher_rows(jax.random.fold_in(splits[16], 71), 0),
    }


@jax.custom_vjp
def low(v):
    return lax.optimization_barrier(v.astype(jnp.bfloat16)).astype(jnp.float32)

@jax.custom_vjp
def low_back(v):
    return v

def low_keep(v):
    return (low(v), None)

def low_pass(kept, grad):
    return (grad,)

def back_keep(v):
    return (v, None)

def back_low(kept, grad):
    return (low(grad),)
low.defvjp(low_keep, low_pass)
low_back.defvjp(back_keep, back_low)
EPS = 1e-05
MASKED = -1e+30
HIGH = lax.Precision.HIGHEST

def binarize(latent, over_axis):
    column_scale = lax.optimization_barrier(jnp.mean(jnp.abs(latent), axis=over_axis, keepdims=True))
    return low(column_scale * jnp.sign(latent))

def layer_norm(features, gain_row, bias_row):
    centre = lax.optimization_barrier(jnp.mean(features, axis=-1, keepdims=True))
    centred = features - centre
    spread = lax.optimization_barrier(jnp.mean(centred * centred, axis=-1, keepdims=True))
    return centred * lax.rsqrt(spread + EPS) * gain_row + bias_row

def attend(queries, key_heads, value_heads, length):
    scores = low_back(jnp.einsum('qhd,khd->hqk', queries, key_heads, precision=HIGH))
    positions = jnp.arange(LEN)
    allowed = (positions[None, :] < length) | (positions[None, :] <= positions[:, None])
    scores = jnp.where(allowed[None], scores, MASKED)
    row_top = lax.optimization_barrier(jnp.max(scores, axis=-1, keepdims=True))
    log_total = row_top + jnp.log(lax.optimization_barrier(jnp.sum(jnp.exp(scores - row_top), axis=-1, keepdims=True)))
    attn_probs = low(jnp.exp(scores - log_total))
    return jnp.einsum('hqk,khd->qhd', attn_probs, value_heads, precision=HIGH)

def block_forward(params, inputs, length):
    qkv_w, out_w, up_w, down_w, head_b, up_b, row_table = params
    projected = jnp.einsum('td,jdc->jtc', inputs, qkv_w, precision=HIGH)
    queries = low_back(low((projected[0] + head_b[0]) * (1.0 / math.sqrt(HEAD))))
    key_heads = low_back(low(projected[1]))
    value_heads = low_back(low(projected[2] + head_b[1]))
    head_shape = (LEN, HEADS, HEAD)
    context = attend(queries.reshape(head_shape), key_heads.reshape(head_shape), value_heads.reshape(head_shape), length)
    context = low_back(low(context.reshape(LEN, D)))
    branch = low_back(jnp.dot(context, out_w, precision=HIGH))
    residual_one = inputs + branch + row_table[0]
    hidden = layer_norm(residual_one, row_table[2], row_table[3])
    pre_act = low_back(jnp.dot(low(hidden), up_w, precision=HIGH) + up_b)
    activation = low(jax.nn.gelu(pre_act, approximate=False))
    ffn_out = low_back(jnp.dot(activation, down_w, precision=HIGH))
    return layer_norm(hidden + ffn_out + row_table[1], row_table[4], row_table[5])

def run_layer(params, sequences, prefix):

    def per_sequence(sequence):
        return block_forward(params, sequence[0], sequence[1])
    return lax.map(jax.checkpoint(per_sequence), (sequences, prefix))

def reference(tokens, prefix, qkv_latent, out_latent, up_latent, down_latent, head_bias, up_bias, row_params, teacher_qkv, teacher_out, teacher_up, teacher_down, teacher_head_bias, teacher_up_bias, teacher_rows):
    student_params = (binarize(qkv_latent, 1), binarize(out_latent, 1), binarize(up_latent, 0), binarize(down_latent, 1), head_bias, up_bias, row_params)
    teacher_params = (teacher_qkv.astype(jnp.float32), teacher_out.astype(jnp.float32), teacher_up.astype(jnp.float32), teacher_down.astype(jnp.float32), teacher_head_bias, teacher_up_bias, teacher_rows)
    sequences = tokens.astype(jnp.float32).reshape(SEQS, LEN, D)
    target = run_layer(teacher_params, sequences, prefix)

    def student_fn(params, seq_inputs):
        return run_layer(params, seq_inputs, prefix)
    result, pullback = jax.vjp(student_fn, student_params, sequences)
    gradients, input_grad = pullback(result - target)
    return (result.reshape(TOKENS, D).astype(jnp.bfloat16), input_grad.reshape(TOKENS, D), gradients[0], gradients[1], gradients[2], gradients[3], gradients[4], gradients[5], gradients[6])
```

```python
import math
from functools import partial

import jax
import jax.numpy as jnp
from jax import lax
from jax.experimental import pallas as pl
from jax.experimental.pallas import tpu as pltpu
from jax.sharding import PartitionSpec as P

D = 768
FF = 3072
HEAD = 64
LEN = 2048
HALF_D = D // 2
HALF_F = FF // 2
HALF_L = LEN // 2
PREFIX_MAX = LEN // 2
QB = 256
TB = 256
EPS = 1e-05
MASKED = -1e30
BF = jnp.bfloat16
F32 = jnp.float32
BOTH = ("dp", "tensor")
VMEM_LIMIT = 60 * 1024 * 1024


def nt(a, b):
    return lax.dot_general(a, b, (((1,), (1,)), ((), ())), preferred_element_type=F32)


def nn(a, b):
    return lax.dot_general(a, b, (((1,), (0,)), ((), ())), preferred_element_type=F32)


def tn(a, b):
    return lax.dot_general(a, b, (((0,), (0,)), ((), ())), preferred_element_type=F32)


def swap_route(dp):
    return [(2 * d + t, 2 * d + 1 - t) for d in range(dp) for t in range(2)]


def far_route(dp, k):
    return [(2 * d + t, 2 * (d ^ (4 * k)) + t) for d in range(dp) for t in range(2)]


def near_route(dp, which):
    out = []
    for d in range(dp):
        for t in range(2):
            bit = 2 if (t == 0) == (which == 0) else 1
            out.append((2 * d + t, 2 * (d ^ bit) + t))
    return out


def send(x, route):
    return lax.ppermute(x, BOTH, route)


def gather_pieces(chunk, dp):
    far = dp // 4
    got = [chunk] + [send(chunk, far_route(dp, k)) for k in range(1, far)]
    mine = jnp.concatenate(got, axis=0)
    first = send(mine, near_route(dp, 0))
    second = send(mine, near_route(dp, 1))
    third = send(first, near_route(dp, 1))
    return [mine, first, second, third]


def scatter_pieces(pieces, dp):
    far = dp // 4
    mine, first, second, third = pieces
    rows = mine.shape[0] // far
    third_in = send(third, near_route(dp, 1))
    second_in = send(second, near_route(dp, 1))
    first_sum = (first.astype(F32) + third_in.astype(F32)).astype(BF)
    first_in = send(first_sum, near_route(dp, 0))
    total = [
        mine[k * rows : (k + 1) * rows].astype(F32)
        + first_in[k * rows : (k + 1) * rows].astype(F32)
        + second_in[k * rows : (k + 1) * rows].astype(F32)
        for k in range(far)
    ]
    out = total[0]
    for k in range(1, far):
        out = out + send(total[k].astype(BF), far_route(dp, k)).astype(F32)
    return out


def piece_mask(p, t):
    if p == 0:
        return 0
    if p == 3:
        return 3
    return jnp.where((t == 0) == (p == 1), 2, 1)


def rank_of(ids, t, p, k):
    return lax.bitwise_xor(ids[0], 4 * k + piece_mask(p, t))


def rows_at(start, size):
    return pl.ds(pl.multiple_of(start, 8), size)


def load_chunks(ids, sets, sems):
    copies = []
    for pieces, t, rows, parts in sets:
        if len(pieces) == 1:
            for src, target, base, size in parts:
                copies.append((pieces[0].at[pl.ds(src, size)], target.at[rows_at(base, size)]))
            continue
        for p, piece in enumerate(pieces):
            for k in range(piece.shape[0] // rows):
                r = rank_of(ids, t, p, k)
                for off, size, target, base in parts:
                    copies.append(
                        (
                            piece.at[pl.ds(k * rows + off, size)],
                            target.at[rows_at(base + r * size, size)],
                        )
                    )
    copies = [pltpu.make_async_copy(s, d, sems.at[i]) for i, (s, d) in enumerate(copies)]
    for c in copies:
        c.start()
    for c in copies:
        c.wait()


def count_chunks(sets):
    n = 0
    for pieces, rows, parts in sets:
        n += parts if len(pieces) == 1 else parts * sum(p.shape[0] // rows for p in pieces)
    return n


ANY = pl.BlockSpec(memory_space=pl.ANY)


def params(n=1):
    return pltpu.CompilerParams(
        dimension_semantics=("arbitrary",) * n, vmem_limit_bytes=VMEM_LIMIT
    )


def qkv_kernel(np_, rows, ids, x_own, x_other, bias, *rest):
    pieces, rest = rest[:np_], rest[np_:]
    q_ref, k_ref, v_ref, w_out, w, sems = rest
    i = pl.program_id(0)
    c = rows // 3

    @pl.when(i == 0)
    def _():
        if np_ == 1:
            parts = [(0, w, 0, 3 * HALF_D)]
        else:
            parts = [(j * c, c, w, j * HALF_D) for j in range(3)]
        load_chunks(ids, [(pieces, ids[1], rows, parts)], sems)
        w_out[...] = w[...]

    x = jnp.where(i // 2 == ids[1], x_own[...], x_other[...])
    q_ref[...] = ((nt(x, w[0:HALF_D, :]) + bias[0:1, :]) * (1.0 / math.sqrt(HEAD))).astype(BF)
    k_ref[...] = nt(x, w[HALF_D : 2 * HALF_D, :]).astype(BF)
    v_ref[...] = (nt(x, w[2 * HALF_D :, :]) + bias[1:2, :]).astype(BF)


def project(ids, x_own, x_other, bias, pieces, rows):
    tb = 512
    np_ = len(pieces)
    n = count_chunks([(pieces, rows, 1 if np_ == 1 else 3)])
    xs = pl.BlockSpec((tb, D), lambda i, ids: (i % 2, 0))
    full = pl.BlockSpec((tb, HALF_D), lambda i, ids: (i, 0))
    return pl.pallas_call(
        partial(qkv_kernel, np_, rows),
        out_shape=[jax.ShapeDtypeStruct((LEN, HALF_D), BF)] * 3
        + [jax.ShapeDtypeStruct((3 * HALF_D, D), BF)],
        grid_spec=pltpu.PrefetchScalarGridSpec(
            num_scalar_prefetch=1,
            grid=(LEN // tb,),
            in_specs=[xs, xs, pl.BlockSpec((2, HALF_D), lambda i, ids: (0, 0))] + [ANY] * np_,
            out_specs=[full] * 3 + [pl.BlockSpec((3 * HALF_D, D), lambda i, ids: (0, 0))],
            scratch_shapes=[pltpu.VMEM((3 * HALF_D, D), BF), pltpu.SemaphoreType.DMA((n,))],
        ),
        compiler_params=params(),
        cost_estimate=pl.CostEstimate(
            flops=2 * LEN * 3 * HALF_D * D, transcendentals=0, bytes_accessed=12 << 20
        ),
        name="project",
    )(ids, x_own, x_other, bias, *pieces)


def allowed(prefix, q0, nq, k0, nk, keys_first):
    if k0 + nk - 1 <= q0:
        return None
    shape, ka, qa = ((nk, nq), 0, 1) if keys_first else ((nq, nk), 1, 0)
    kp = k0 + lax.broadcasted_iota(jnp.int32, shape, ka)
    qp = q0 + lax.broadcasted_iota(jnp.int32, shape, qa)
    causal = kp <= qp
    if k0 >= PREFIX_MAX:
        return causal
    if k0 > q0 + nq - 1:
        return kp < prefix
    return causal | (kp < prefix)


def keys_for(q0):
    return max(q0 + QB, PREFIX_MAX)


def attend_kernel(want_log, ids, q_ref, k_ref, v_ref, c_ref, *rest):
    h = lax.rem(pl.program_id(0), 2)
    prefix = ids[2]
    lane = lax.broadcasted_iota(jnp.int32, (QB, 2 * HEAD), 1)
    own = (lane // HEAD) == h
    ones = jnp.ones((LEN, 2 * HEAD), BF)
    vx = jnp.concatenate([v_ref[...], ones], axis=1)
    for q0 in range(0, LEN, QB):
        nk = keys_for(q0)
        q = jnp.where(own, q_ref[q0 : q0 + QB, :], jnp.zeros((), BF))
        flat = (q0 // QB) * QB
        parts = []
        if flat:
            parts.append(nt(q, k_ref[0:flat, :]))
        for k0 in range(flat, nk, QB):
            s = nt(q, k_ref[k0 : k0 + QB, :])
            parts.append(jnp.where(allowed(prefix, q0, QB, k0, QB, False), s, MASKED))
        top = parts[0].max(axis=1, keepdims=True)
        for s in parts[1:]:
            top = jnp.maximum(top, s.max(axis=1, keepdims=True))
        probs = [jnp.exp(s - top).astype(BF) for s in parts]
        probs = probs[0] if len(probs) == 1 else jnp.concatenate(probs, axis=1)
        o = nn(probs, vx[0:nk, :])
        total = o[:, 2 * HEAD :]
        ctx = (o[:, : 2 * HEAD] / total).astype(BF)
        half = lax.rem(q0 // HALF_L + ids[1], 2)
        at = pl.ds(q0 % HALF_L, QB)
        c_ref[half, at, :] = jnp.where(own | (h == 0), ctx, c_ref[half, at, :])
        if want_log:
            log_total = top + jnp.log(total)
            rest[0][0, h, :, q0 : q0 + QB] = jnp.transpose(log_total)[0:8, :]


def attend(ids, q, k, v, want_log):
    heads = HALF_D // HEAD
    pair = pl.BlockSpec((LEN, 2 * HEAD), lambda p, ids: (0, p // 2))
    outs = [jax.ShapeDtypeStruct((2, HALF_L, HALF_D), BF)]
    specs = [pl.BlockSpec((2, HALF_L, 2 * HEAD), lambda p, ids: (0, 0, p // 2))]
    if want_log:
        outs.append(jax.ShapeDtypeStruct((heads // 2, 2, 8, LEN), F32))
        specs.append(pl.BlockSpec((1, 2, 8, LEN), lambda p, ids: (p // 2, 0, 0, 0)))
    return pl.pallas_call(
        partial(attend_kernel, want_log),
        out_shape=outs,
        grid_spec=pltpu.PrefetchScalarGridSpec(
            num_scalar_prefetch=1, grid=(heads,), in_specs=[pair] * 3, out_specs=specs
        ),
        compiler_params=params(),
        cost_estimate=pl.CostEstimate(
            flops=16 << 30, transcendentals=heads * LEN * LEN // 2, bytes_accessed=6 << 20
        ),
        name="attend",
    )(ids, q, k, v)


def attend_back_kernel(
    ids, q_ref, k_ref, v_ref, c_ref, go_ref, gx_ref, log_ref, gq_ref, gk_ref, gv_ref,
    g_all, mid_all, qt, kacc, vacc
):
    h = lax.rem(pl.program_id(0), 2)
    prefix, t = ids[2], ids[1]
    lane = lax.broadcasted_iota(jnp.int32, (HALF_L, 2 * HEAD), 1)
    own = (lane // HEAD) == h
    zero = jnp.zeros((), BF)
    for half, ref in ((0, go_ref), (1, gx_ref)):
        g = jnp.where(own, ref[...], zero)
        at = pl.ds(pl.multiple_of(lax.rem(t + half, 2) * HALF_L, HALF_L), HALF_L)
        g_all[at, :] = g
        mid = jnp.sum(g.astype(F32) * c_ref[half].astype(F32), axis=1, keepdims=True)
        mid_all[:, at] = jnp.transpose(jnp.broadcast_to(mid, (HALF_L, 2 * HEAD)))[0:8, :]

    @pl.when(h == 0)
    def _():
        qt[...] = jnp.zeros_like(qt)
        kacc[...] = jnp.zeros_like(kacc)
        vacc[...] = jnp.zeros_like(vacc)

    kb = QB
    own_k = (lax.broadcasted_iota(jnp.int32, (kb, 2 * HEAD), 1) // HEAD) == h
    own_q = (lax.broadcasted_iota(jnp.int32, (LEN, 2 * HEAD), 1) // HEAD) == h
    q_all = jnp.where(own_q, q_ref[...], zero)
    for k0 in range(0, LEN, kb):
        k_blk = jnp.where(own_k, k_ref[k0 : k0 + kb, :], zero)
        v_blk = v_ref[k0 : k0 + kb, :]
        q0 = 0 if k0 < PREFIX_MAX else k0
        nq = LEN - q0
        s = nt(k_blk, q_all[q0:, :])
        flat = k0 + kb
        parts = []
        for c0 in range(q0, flat, QB):
            m = allowed(prefix, c0, QB, k0, kb, True)
            parts.append(jnp.where(m, s[:, c0 - q0 : c0 - q0 + QB], MASKED))
        if flat < LEN:
            parts.append(s[:, flat - q0 :])
        s = parts[0] if len(parts) == 1 else jnp.concatenate(parts, axis=1)
        p = jnp.exp(s - log_ref[0, h, 0:1, q0:])
        g = g_all[q0:, :]
        gp = nt(v_blk, g)
        gs = (p * (gp - mid_all[0:1, q0:])).astype(BF)
        vacc[k0 : k0 + kb, :] += nn(p.astype(BF), g)
        kacc[k0 : k0 + kb, :] += nn(gs, q_all[q0:, :])
        qt[:, q0:] += tn(k_blk, gs)

    @pl.when(h == 1)
    def _():
        gq_ref[...] = jnp.transpose(qt[...]).astype(BF)
        gk_ref[...] = kacc[...].astype(BF)
        gv_ref[...] = vacc[...].astype(BF)


def attend_back(ids, q, k, v, ctx, g_own, g_other, logs):
    heads = HALF_D // HEAD
    pair = pl.BlockSpec((LEN, 2 * HEAD), lambda p, ids: (0, p // 2))
    half = pl.BlockSpec((HALF_L, 2 * HEAD), lambda p, ids: (0, p // 2))
    return pl.pallas_call(
        attend_back_kernel,
        out_shape=[jax.ShapeDtypeStruct((LEN, HALF_D), BF)] * 3,
        grid_spec=pltpu.PrefetchScalarGridSpec(
            num_scalar_prefetch=1,
            grid=(heads,),
            in_specs=[pair] * 3
            + [pl.BlockSpec((2, HALF_L, 2 * HEAD), lambda p, ids: (0, 0, p // 2))]
            + [half] * 2
            + [pl.BlockSpec((1, 2, 8, LEN), lambda p, ids: (p // 2, 0, 0, 0))],
            out_specs=[pair] * 3,
            scratch_shapes=[
                pltpu.VMEM((LEN, 2 * HEAD), BF),
                pltpu.VMEM((8, LEN), F32),
                pltpu.VMEM((2 * HEAD, LEN), F32),
                pltpu.VMEM((LEN, 2 * HEAD), F32),
                pltpu.VMEM((LEN, 2 * HEAD), F32),
            ],
        ),
        compiler_params=params(),
        cost_estimate=pl.CostEstimate(
            flops=40 << 30, transcendentals=heads * LEN * LEN // 2, bytes_accessed=10 << 20
        ),
        name="attend_back",
    )(ids, q, k, v, ctx, g_own, g_other, logs)


def norm(v):
    centred = v - jnp.mean(v, axis=-1, keepdims=True)
    r = lax.rsqrt(jnp.mean(centred * centred, axis=-1, keepdims=True) + EPS)
    return centred * r, r


def norm_back(g, n, r, gain):
    gn = g * gain
    return r * (
        gn - jnp.mean(gn, axis=-1, keepdims=True) - n * jnp.mean(gn * n, axis=-1, keepdims=True)
    )


INV_ROOT2 = 1.0 / math.sqrt(2.0)
INV_ROOT2PI = 1.0 / math.sqrt(2.0 * math.pi)
FC = 768


def load_layer(ids, np_, rows, own, other, up, down, out, sems):
    if np_ == 1:
        t = ids[1]

        def parts(side):
            return [
                (0, up, side * HALF_F, HALF_F),
                (HALF_F, down, side * HALF_F, HALF_F),
                (2 * HALF_F, out, side * HALF_D, HALF_D),
            ]
    else:
        t = ids[1]
        c = (rows * HALF_D) // (2 * HALF_F + HALF_D)
        f = (rows - c) // 2

        def parts(side):
            return [
                (0, f, up, side * HALF_F),
                (f, f, down, side * HALF_F),
                (2 * f, c, out, side * HALF_D),
            ]

    load_chunks(ids, [(own, t, rows, parts(t)), (other, 1 - t, rows, parts(1 - t))], sems)


def branch(ids, x, c_own, c_other, out, bias):
    t = ids[1]
    o = nn(c_own, out[rows_at(t * HALF_D, HALF_D), :])
    o = o + nn(c_other, out[rows_at((1 - t) * HALF_D, HALF_D), :])
    return x.astype(F32) + o + bias


def teacher_kernel(np_, rows, ids, x, c_own, c_other, row, unit, *rest):
    own, other, rest = rest[:np_], rest[np_ : 2 * np_], rest[2 * np_ :]
    y, up, down, out, sems = rest

    @pl.when(pl.program_id(0) == 0)
    def _():
        load_layer(ids, np_, rows, own, other, up, down, out, sems)

    mixed = branch(ids, x[...], c_own[0], c_other[...], out, row[0:1, :])
    hidden = norm(mixed)[0] * row[2:3, :] + row[3:4, :]
    hb = hidden.astype(BF)
    total = hidden + row[1:2, :]
    for f in range(0, FF, FC):
        pre = nt(hb, up[f : f + FC, :]) + unit[0:1, f : f + FC]
        act = (pre * (0.5 + 0.5 * lax.erf(pre * INV_ROOT2))).astype(BF)
        total = total + nn(act, down[f : f + FC, :])
    y[...] = norm(total)[0] * row[4:5, :] + row[5:6, :]


def layer_scratch(own, rows):
    n = 2 * count_chunks([(own, rows, 3)])
    return [
        pltpu.VMEM((FF, D), BF),
        pltpu.VMEM((FF, D), BF),
        pltpu.VMEM((D, D), BF),
        pltpu.SemaphoreType.DMA((n,)),
    ]


def block(cols):
    return pl.BlockSpec((TB, cols), lambda i, ids: (i, 0))


def whole(*shape):
    return pl.BlockSpec(shape, lambda i, ids: (0,) * len(shape))


FIRST_HALF = pl.BlockSpec((1, TB, HALF_D), lambda i, ids: (0, i, 0))


def teacher_ffn(ids, x, ctx, c_other, row, unit, own, other, rows):
    tokens = x.shape[0]
    np_ = len(own)
    return pl.pallas_call(
        partial(teacher_kernel, np_, rows),
        out_shape=jax.ShapeDtypeStruct((tokens, D), F32),
        grid_spec=pltpu.PrefetchScalarGridSpec(
            num_scalar_prefetch=1,
            grid=(tokens // TB,),
            in_specs=[block(D), FIRST_HALF, block(HALF_D), whole(6, D), whole(1, FF)]
            + [ANY] * (2 * np_),
            out_specs=block(D),
            scratch_shapes=layer_scratch(own, rows),
        ),
        compiler_params=params(),
        cost_estimate=pl.CostEstimate(
            flops=2 * tokens * D * (2 * FF + D), transcendentals=tokens * FF, bytes_accessed=16 << 20
        ),
        name="teacher_ffn",
    )(ids, x, ctx, c_other, row, unit, *own, *other)


def student_kernel(np_, rows, ids, x, c_own, c_other, y, row, unit, *rest):
    own, other, rest = rest[:np_], rest[np_ : 2 * np_], rest[2 * np_ :]
    (
        student, act_ref, gpre_ref, hid_ref, gffn_ref, gbr_ref, gmix_ref, gown_ref, gother_ref,
        sums, unit_sums, up, down, out, sems, slope
    ) = rest
    i = pl.program_id(0)

    @pl.when(i == 0)
    def _():
        load_layer(ids, np_, rows, own, other, up, down, out, sems)
        sums[...] = jnp.zeros_like(sums)
        unit_sums[...] = jnp.zeros_like(unit_sums)

    mixed = branch(ids, x[...], c_own[0], c_other[...], out, row[0:1, :])
    n1, r1 = norm(mixed)
    hidden = n1 * row[2:3, :] + row[3:4, :]
    hb = hidden.astype(BF)
    hid_ref[...] = hb
    total = hidden + row[1:2, :]
    for f in range(0, FF, FC):
        pre = nt(hb, up[f : f + FC, :]) + unit[0:1, f : f + FC]
        phi = 0.5 + 0.5 * lax.erf(pre * INV_ROOT2)
        act = (pre * phi).astype(BF)
        slope[:, f : f + FC] = phi + pre * (jnp.exp(pre * pre * -0.5) * INV_ROOT2PI)
        act_ref[:, f : f + FC] = act
        total = total + nn(act, down[f : f + FC, :])
    n2, r2 = norm(total)
    result = n2 * row[4:5, :] + row[5:6, :]
    student[...] = result.astype(BF)
    diff = result - y[...]
    gsum = norm_back(diff, n2, r2, row[4:5, :])
    gffn = gsum.astype(BF)
    gffn_ref[...] = gffn
    ghid = gsum
    for f in range(0, FF, FC):
        gact = nt(gffn, down[f : f + FC, :])
        gpre = (gact * slope[:, f : f + FC]).astype(BF)
        gpre_ref[:, f : f + FC] = gpre
        unit_sums[0:1, f : f + FC] += jnp.sum(gpre.astype(F32), axis=0, keepdims=True)
        ghid = ghid + nn(gpre, up[f : f + FC, :])
    gmix = norm_back(ghid, n1, r1, row[2:3, :])
    gmix_ref[...] = gmix
    gbr = gmix.astype(BF)
    gbr_ref[...] = gbr
    t = ids[1]
    gown_ref[...] = nt(gbr, out[rows_at(t * HALF_D, HALF_D), :]).astype(BF)
    gother_ref[...] = nt(gbr, out[rows_at((1 - t) * HALF_D, HALF_D), :]).astype(BF)
    for j, term in enumerate((gmix, gsum, ghid * n1, ghid, diff * n2, diff)):
        sums[j : j + 1, :] += jnp.sum(term, axis=0, keepdims=True)


def student_ffn(ids, x, ctx, c_other, y, row, unit, own, other, rows):
    tokens = x.shape[0]
    np_ = len(own)
    s = jax.ShapeDtypeStruct
    return pl.pallas_call(
        partial(student_kernel, np_, rows),
        out_shape=[
            s((tokens, D), BF),
            s((tokens, FF), BF),
            s((tokens, FF), BF),
            s((tokens, D), BF),
            s((tokens, D), BF),
            s((tokens, D), BF),
            s((tokens, D), F32),
            s((tokens, HALF_D), BF),
            s((tokens, HALF_D), BF),
            s((8, D), F32),
            s((8, FF), F32),
        ],
        grid_spec=pltpu.PrefetchScalarGridSpec(
            num_scalar_prefetch=1,
            grid=(tokens // TB,),
            in_specs=[block(D), FIRST_HALF, block(HALF_D), block(D), whole(6, D), whole(1, FF)]
            + [ANY] * (2 * np_),
            out_specs=[
                block(D), block(FF), block(FF), block(D), block(D), block(D), block(D),
                block(HALF_D), block(HALF_D), whole(8, D), whole(8, FF),
            ],
            scratch_shapes=layer_scratch(own, rows) + [pltpu.VMEM((TB, FF), F32)],
        ),
        compiler_params=params(),
        cost_estimate=pl.CostEstimate(
            flops=2 * tokens * D * (4 * FF + 2 * D),
            transcendentals=2 * tokens * FF,
            bytes_accessed=40 << 20,
        ),
        name="student_ffn",
    )(ids, x, ctx, c_other, y, row, unit, *own, *other)


def store_chunks(ids, side_t, far, rows, outs, off, size, acc, ranks):
    for j, first in ranks:
        k = lax.bitwise_xor(ids[0] // 4, j)
        for p in range(4):
            sub = lax.bitwise_xor(lax.rem(ids[0], 4), piece_mask(p, side_t))
            value = acc[rows_at((first + sub) * size, size), :].astype(BF)
            outs[p][rows_at(k * rows + off, size), :] = value


def ffn_grad_kernel(flat, far, rows, own_side, ids, act, gpre, ctx, hid, gffn, gbr, *rest):
    outs, (acc,) = rest[:-1], rest[-1:]
    i = pl.program_id(0)
    side_t = ids[1] if own_side else 1 - ids[1]
    per = acc.shape[0]
    if flat:
        up_out, down_out, out_out = outs
        up_out[...] = tn(gpre[...], hid[...])
        down_out[...] = tn(act[...], gffn[...])

        @pl.when(i == 0)
        def _():
            out_out[...] = tn(ctx[...], gbr[...])

        return
    c = (rows * HALF_D) // (2 * HALF_F + HALF_D)
    f = (rows - c) // 2
    groups = per // (4 * f)
    for off, lhs, rhs in ((0, gpre, hid), (f, act, gffn)):
        acc[...] = tn(lhs[...], rhs[...])
        store_chunks(
            ids, side_t, far, rows, outs, off, f, acc,
            [(i * groups + j, 4 * j) for j in range(groups)]
        )

    @pl.when(i == 0)
    def _():
        acc[0:HALF_D, :] = tn(ctx[...], gbr[...])
        store_chunks(
            ids, side_t, far, rows, outs, 2 * f, c, acc, [(j, 4 * j) for j in range(far)]
        )


def ffn_grads(ids, act, gpre, ctx, hid, gffn, gbr, rows, dp, fast, own_side):
    tokens = hid.shape[0]
    far = dp // 4
    fb = HALF_D
    steps = HALF_F // fb

    def col(i, ids):
        side = ids[1] if own_side else 1 - ids[1]
        return (0, side * steps + i)

    if fast:
        out_shape = [jax.ShapeDtypeStruct((far * rows, D), BF)] * 4
        out_specs = [whole(far * rows, D)] * 4
    else:
        out_shape = [
            jax.ShapeDtypeStruct((HALF_F, D), F32),
            jax.ShapeDtypeStruct((HALF_F, D), F32),
            jax.ShapeDtypeStruct((HALF_D, D), F32),
        ]
        cols = pl.BlockSpec((fb, D), lambda i, ids: (i, 0))
        out_specs = [cols, cols, whole(HALF_D, D)]
    return pl.pallas_call(
        partial(ffn_grad_kernel, not fast, far, rows, own_side),
        out_shape=out_shape,
        grid_spec=pltpu.PrefetchScalarGridSpec(
            num_scalar_prefetch=1,
            grid=(steps,),
            in_specs=[
                pl.BlockSpec((tokens, fb), col),
                pl.BlockSpec((tokens, fb), col),
                whole(tokens, HALF_D),
                whole(tokens, D),
                whole(tokens, D),
                whole(tokens, D),
            ],
            out_specs=out_specs,
            scratch_shapes=[pltpu.VMEM((fb, D), F32)],
        ),
        compiler_params=params(),
        cost_estimate=pl.CostEstimate(
            flops=2 * tokens * D * (FF + HALF_D), transcendentals=0, bytes_accessed=16 << 20
        ),
        name="ffn_grads",
    )(ids, act, gpre, ctx, hid, gffn, gbr)


def qkv_grad_kernel(flat, far, rows, ids, gq, gk, gv, x_own, x_other, *rest):
    outs, (x_all, acc) = rest[:-2], rest[-2:]
    i = pl.program_id(0)
    t = ids[1]

    @pl.when(i == 0)
    def _():
        x_all[rows_at(t * HALF_L, HALF_L), :] = x_own[...]
        x_all[rows_at((1 - t) * HALF_L, HALF_L), :] = x_other[...]

    c = rows // 3
    for j, g in enumerate((gq, gk, gv)):

        @pl.when(i == j)
        def _():
            value = tn(g[...], x_all[...])
            if j == 0:
                value = value * (1.0 / math.sqrt(HEAD))
            if flat:
                outs[0][j * HALF_D : (j + 1) * HALF_D, :] = value
            else:
                acc[...] = value
                store_chunks(
                    ids, t, far, rows, outs, j * c, c, acc, [(r, 4 * r) for r in range(far)]
                )


def qkv_grads(ids, gq, gk, gv, x_own, x_other, rows, dp, fast):
    far = dp // 4
    if fast:
        out_shape = [jax.ShapeDtypeStruct((far * rows, D), BF)] * 4
        out_specs = [whole(far * rows, D)] * 4
    else:
        out_shape = [jax.ShapeDtypeStruct((3 * HALF_D, D), F32)]
        out_specs = [whole(3 * HALF_D, D)]
    return pl.pallas_call(
        partial(qkv_grad_kernel, not fast, far, rows),
        out_shape=out_shape,
        grid_spec=pltpu.PrefetchScalarGridSpec(
            num_scalar_prefetch=1,
            grid=(3,),
            in_specs=[whole(LEN, HALF_D)] * 3 + [whole(HALF_L, D)] * 2,
            out_specs=out_specs,
            scratch_shapes=[pltpu.VMEM((LEN, D), BF), pltpu.VMEM((HALF_D, D), F32)],
        ),
        compiler_params=params(),
        cost_estimate=pl.CostEstimate(
            flops=2 * LEN * 3 * HALF_D * D, transcendentals=0, bytes_accessed=10 << 20
        ),
        name="qkv_grads",
    )(ids, gq, gk, gv, x_own, x_other)


def binarize(latent, over_axis):
    scale = jnp.mean(jnp.abs(latent), axis=over_axis, keepdims=True)
    return (scale * jnp.sign(latent)).astype(BF)


def local(
    tokens, prefix, qkv_latent, out_latent, up_latent, down_latent, head_bias, up_bias, row_params,
    teacher_qkv, teacher_out, teacher_up, teacher_down, teacher_head_bias, teacher_up_bias,
    teacher_rows,
):
    dp = lax.axis_size("dp")
    n_dev = 2 * dp
    c = qkv_latent.shape[2]
    f = up_latent.shape[1]
    fast = c % 8 == 0 and dp % 4 == 0
    dp_rank = lax.axis_index("dp").astype(jnp.int32)
    t = lax.axis_index("tensor").astype(jnp.int32)
    ids = jnp.stack([dp_rank, t, prefix[0]])

    def qkv_rows(w):
        return jnp.transpose(w, (0, 2, 1)).reshape(3 * c, D)

    def rest_rows(up, down, out):
        return jnp.concatenate([jnp.transpose(up), down, out], axis=0)

    student_a = qkv_rows(binarize(qkv_latent, 1))
    teacher_a = qkv_rows(teacher_qkv)
    student_b = rest_rows(binarize(up_latent, 0), binarize(down_latent, 1), binarize(out_latent, 1))
    teacher_b = rest_rows(teacher_up, teacher_down, teacher_out)

    def small(hb, ub, rp):
        return [hb.reshape(-1), ub, rp.reshape(-1)]

    smalls = jnp.concatenate(
        small(head_bias, up_bias, row_params)
        + small(teacher_head_bias, teacher_up_bias, teacher_rows)
    )
    n_small = smalls.shape[0] // 2
    smalls = lax.all_to_all(jnp.broadcast_to(smalls, (n_dev, 2 * n_small)), BOTH, 0, 0)

    def unpack(part):
        hb = part[:, : 2 * c].reshape(n_dev, 2, c).transpose(1, 0, 2).reshape(2, D)
        ub = part[:, 2 * c : 2 * c + f].reshape(1, FF)
        rp = part[:, 2 * c + f :].reshape(n_dev, 6, c).transpose(1, 0, 2).reshape(6, D)
        return lax.dynamic_slice_in_dim(hb, t * HALF_D, HALF_D, 1), ub, rp

    s_head, s_unit, s_row = unpack(smalls[:, :n_small])
    t_head, t_unit, t_row = unpack(smalls[:, n_small:])

    x_other = send(tokens, swap_route(dp))

    if fast:
        a_rows, b_rows = 3 * c, 2 * f + c
        pieces_sa = gather_pieces(student_a, dp)
        pieces_ta = gather_pieces(teacher_a, dp)
        pieces_tb = gather_pieces(teacher_b, dp)
        pieces_sb = gather_pieces(student_b, dp)
        others_tb = [send(p, swap_route(dp)) for p in pieces_tb]
        others_sb = [send(p, swap_route(dp)) for p in pieces_sb]
    else:

        def gathered(x, sizes):
            parts, at = [], 0
            for n in sizes:
                parts.append(lax.all_gather(x[at : at + n], "dp", axis=0, tiled=True))
                at += n
            return [jnp.concatenate(parts, axis=0)]

        a_rows, b_rows = 3 * HALF_D, 2 * HALF_F + HALF_D
        pieces_sa = gathered(student_a, (c, c, c))
        pieces_ta = gathered(teacher_a, (c, c, c))
        pieces_tb = gathered(teacher_b, (f, f, c))
        pieces_sb = gathered(student_b, (f, f, c))
        others_tb = [send(p, swap_route(dp)) for p in pieces_tb]
        others_sb = [send(p, swap_route(dp)) for p in pieces_sb]

    q, k, v, w_qkv = project(ids, tokens, x_other, s_head, pieces_sa, a_rows)
    ctx, logs = attend(ids, q, k, v, True)
    ctx_other = send(ctx[1], swap_route(dp))
    tq, tk, tv, _ = project(ids, tokens, x_other, t_head, pieces_ta, a_rows)
    t_ctx = attend(ids, tq, tk, tv, False)[0]
    t_other = send(t_ctx[1], swap_route(dp))

    y = teacher_ffn(ids, tokens, t_ctx, t_other, t_row, t_unit, pieces_tb, others_tb, b_rows)
    (student, act, gpre, hid, gffn, gbr, gmix, g_own, g_send, sums, unit_sums) = student_ffn(
        ids, tokens, ctx, ctx_other, y, s_row, s_unit, pieces_sb, others_sb, b_rows
    )
    g_other = send(g_send, swap_route(dp))

    away = ffn_grads(ids, act, gpre, ctx_other, hid, gffn, gbr, b_rows, dp, fast, False)
    away = [send(p, swap_route(dp)) for p in away]
    home = ffn_grads(ids, act, gpre, ctx[0], hid, gffn, gbr, b_rows, dp, fast, True)
    if fast:
        home = [(a.astype(F32) + b.astype(F32)).astype(BF) for a, b in zip(home, away)]
        b_grad = scatter_pieces(home, dp)
        up_grad, down_grad, out_grad = b_grad[:f], b_grad[f : 2 * f], b_grad[2 * f :]
    else:
        up_grad, down_grad, out_grad = [
            lax.psum_scatter(a + b, "dp", scatter_dimension=0, tiled=True)
            for a, b in zip(home, away)
        ]

    gq, gk, gv = attend_back(ids, q, k, v, ctx, g_own, g_other, logs)
    a_pieces = qkv_grads(ids, gq, gk, gv, tokens, x_other, a_rows, dp, fast)
    if fast:
        a_grad = scatter_pieces(a_pieces, dp)
        qkv_grad = a_grad.reshape(3, c, D)
    else:
        qkv_grad = lax.psum_scatter(
            a_pieces[0].reshape(3, HALF_D, D), "dp", scatter_dimension=1, tiled=True
        )

    scale = 1.0 / math.sqrt(HEAD)
    grads = jnp.concatenate([gq * jnp.asarray(scale, BF), gk, gv], axis=1)
    theirs = lax.dynamic_slice_in_dim(grads, (1 - t) * HALF_L, HALF_L, 0)
    ours = lax.dynamic_slice_in_dim(grads, t * HALF_L, HALF_L, 0)
    back_other = send(nn(theirs, w_qkv).astype(BF), swap_route(dp))
    token_grad = gmix + nn(ours, w_qkv) + back_other.astype(F32)

    head_sums = jnp.stack(
        [jnp.sum(gq.astype(F32), axis=0) * scale, jnp.sum(gv.astype(F32), axis=0)]
    )
    head_sums = lax.dynamic_update_slice_in_dim(
        jnp.zeros((2, D), F32), head_sums, t * HALF_D, 1
    )
    small_grads = jnp.concatenate(
        [
            head_sums.reshape(2, n_dev, c).transpose(1, 0, 2).reshape(n_dev, 2 * c),
            unit_sums[0].reshape(n_dev, f),
            sums[:6].reshape(6, n_dev, c).transpose(1, 0, 2).reshape(n_dev, 6 * c),
        ],
        axis=1,
    )
    small_grads = jnp.sum(lax.all_to_all(small_grads, BOTH, 0, 0), axis=0)

    return (
        student,
        token_grad,
        jnp.transpose(qkv_grad, (0, 2, 1)),
        out_grad,
        jnp.transpose(up_grad),
        down_grad,
        small_grads[: 2 * c].reshape(2, c),
        small_grads[2 * c : 2 * c + f],
        small_grads[2 * c + f :].reshape(6, c),
    )


def solution(mesh):
    both, weight = ("dp", "tensor"), ("tensor", "dp")
    params_spec = (
        P(None, None, weight),
        P(weight, None),
        P(None, weight),
        P(weight, None),
        P(None, both),
        P(both),
        P(None, both),
    )
    return jax.shard_map(
        local,
        mesh=mesh,
        in_specs=(P(both, None), P("dp")) + params_spec + params_spec,
        out_specs=(P(both, None), P(both, None)) + params_spec,
        check_vma=False,
    )
```

```python
import math
from functools import partial

import jax
import jax.numpy as jnp
from jax import lax
from jax.experimental import pallas as pl
from jax.experimental.pallas import tpu as pltpu
from jax.sharding import PartitionSpec as P

D = 768
FF = 3072
HEAD = 64
LEN = 2048
HALF_D = D // 2
HALF_F = FF // 2
HALF_L = LEN // 2
PREFIX_MAX = LEN // 2
QB = 256
TB = 256
EPS = 1e-05
MASKED = -1e30
BF = jnp.bfloat16
F32 = jnp.float32
BOTH = ("dp", "tensor")
VMEM_LIMIT = 60 * 1024 * 1024


def nt(a, b):
    return lax.dot_general(a, b, (((1,), (1,)), ((), ())), preferred_element_type=F32)


def nn(a, b):
    return lax.dot_general(a, b, (((1,), (0,)), ((), ())), preferred_element_type=F32)


def tn(a, b):
    return lax.dot_general(a, b, (((0,), (0,)), ((), ())), preferred_element_type=F32)


def swap_route(dp):
    return [(2 * d + t, 2 * d + 1 - t) for d in range(dp) for t in range(2)]


def far_route(dp, k):
    return [(2 * d + t, 2 * (d ^ (4 * k)) + t) for d in range(dp) for t in range(2)]


def near_route(dp, which):
    out = []
    for d in range(dp):
        for t in range(2):
            bit = 2 if (t == 0) == (which == 0) else 1
            out.append((2 * d + t, 2 * (d ^ bit) + t))
    return out


def send(x, route):
    return lax.ppermute(x, BOTH, route)


def far_gather(chunk, dp):
    return jnp.concatenate(
        [chunk] + [send(chunk, far_route(dp, k)) for k in range(1, dp // 4)], axis=0
    )


def far_step(x, dp, k):
    return send(x, far_route(dp, k))


def join(a, b):
    return jnp.concatenate([a, b], axis=0)


def near_a(x, dp):
    return send(x, near_route(dp, 0))


def near_b(x, dp):
    return send(x, near_route(dp, 1))


def swap(x, dp):
    return send(x, swap_route(dp))


def plus(*xs):
    out = xs[0].astype(F32)
    for x in xs[1:]:
        out = out + x.astype(F32)
    return out


def direct_sum(total, dp):
    far = dp // 4
    rows = total.shape[0] // far
    parts = [total[k * rows : (k + 1) * rows] for k in range(far)]
    return plus(
        parts[0], *[far_step(parts[k].astype(BF), dp, k) for k in range(1, far)]
    )


def tie(*xs):
    return lax.optimization_barrier(xs)


def piece_mask(p, t):
    if p == 0:
        return 0
    if p == 3:
        return 3
    return jnp.where((t == 0) == (p == 1), 2, 1)


def rank_of(ids, t, p, k):
    return lax.bitwise_xor(ids[0], 4 * k + piece_mask(p, t))


def rows_at(start, size):
    return pl.ds(pl.multiple_of(start, 8), size)


def load_chunks(ids, sets, sems):
    copies = []
    for pieces, t, rows, parts in sets:
        if len(pieces) == 1:
            for src, target, base, size in parts:
                copies.append((pieces[0].at[pl.ds(src, size)], target.at[rows_at(base, size)]))
            continue
        for p, piece in enumerate(pieces):
            far = piece.shape[0] // rows // 2
            for k in range(2 * far):
                r = rank_of(ids, t, 2 * p + k // far, k % far)
                for off, size, target, base in parts:
                    copies.append(
                        (
                            piece.at[pl.ds(k * rows + off, size)],
                            target.at[rows_at(base + r * size, size)],
                        )
                    )
    copies = [pltpu.make_async_copy(s, d, sems.at[i]) for i, (s, d) in enumerate(copies)]
    for c in copies:
        c.start()
    for c in copies:
        c.wait()


def count_chunks(sets):
    n = 0
    for pieces, rows, parts in sets:
        n += parts if len(pieces) == 1 else parts * sum(p.shape[0] // rows for p in pieces)
    return n


ANY = pl.BlockSpec(memory_space=pl.ANY)


def params(n=1):
    return pltpu.CompilerParams(
        dimension_semantics=("arbitrary",) * n, vmem_limit_bytes=VMEM_LIMIT
    )


def qkv_kernel(np_, rows, ids, x_own, x_other, bias, *rest):
    pieces, rest = rest[:np_], rest[np_:]
    q_ref, k_ref, v_ref, w_out, w, sems = rest
    i = pl.program_id(0)
    c = rows // 3

    @pl.when(i == 0)
    def _():
        if np_ == 1:
            parts = [(0, w, 0, 3 * HALF_D)]
        else:
            parts = [(j * c, c, w, j * HALF_D) for j in range(3)]
        load_chunks(ids, [(pieces, ids[1], rows, parts)], sems)
        w_out[...] = w[...]

    x = jnp.where(i // 2 == ids[1], x_own[...], x_other[...])
    q_ref[...] = ((nt(x, w[0:HALF_D, :]) + bias[0:1, :]) * (1.0 / math.sqrt(HEAD))).astype(BF)
    k_ref[...] = nt(x, w[HALF_D : 2 * HALF_D, :]).astype(BF)
    v_ref[...] = (nt(x, w[2 * HALF_D :, :]) + bias[1:2, :]).astype(BF)


def project(ids, x_own, x_other, bias, pieces, rows):
    tb = 512
    np_ = len(pieces)
    n = count_chunks([(pieces, rows, 1 if np_ == 1 else 3)])
    xs = pl.BlockSpec((tb, D), lambda i, ids: (i % 2, 0))
    full = pl.BlockSpec((tb, HALF_D), lambda i, ids: (i, 0))
    return pl.pallas_call(
        partial(qkv_kernel, np_, rows),
        out_shape=[jax.ShapeDtypeStruct((LEN, HALF_D), BF)] * 3
        + [jax.ShapeDtypeStruct((3 * HALF_D, D), BF)],
        grid_spec=pltpu.PrefetchScalarGridSpec(
            num_scalar_prefetch=1,
            grid=(LEN // tb,),
            in_specs=[xs, xs, pl.BlockSpec((2, HALF_D), lambda i, ids: (0, 0))] + [ANY] * np_,
            out_specs=[full] * 3 + [pl.BlockSpec((3 * HALF_D, D), lambda i, ids: (0, 0))],
            scratch_shapes=[pltpu.VMEM((3 * HALF_D, D), BF), pltpu.SemaphoreType.DMA((n,))],
        ),
        compiler_params=params(),
        cost_estimate=pl.CostEstimate(
            flops=2 * LEN * 3 * HALF_D * D, transcendentals=0, bytes_accessed=12 << 20
        ),
        name="project",
    )(ids, x_own, x_other, bias, *pieces)


def allowed(prefix, q0, nq, k0, nk, keys_first):
    if k0 + nk - 1 <= q0:
        return None
    shape, ka, qa = ((nk, nq), 0, 1) if keys_first else ((nq, nk), 1, 0)
    kp = k0 + lax.broadcasted_iota(jnp.int32, shape, ka)
    qp = q0 + lax.broadcasted_iota(jnp.int32, shape, qa)
    causal = kp <= qp
    if k0 >= PREFIX_MAX:
        return causal
    if k0 > q0 + nq - 1:
        return kp < prefix
    return causal | (kp < prefix)


def keys_for(q0):
    return max(q0 + QB, PREFIX_MAX)


def attend_kernel(want_log, ids, q_ref, k_ref, v_ref, c_ref, *rest):
    h = lax.rem(pl.program_id(0), 2)
    prefix = ids[2]
    lane = lax.broadcasted_iota(jnp.int32, (QB, 2 * HEAD), 1)
    own = (lane // HEAD) == h
    ones = jnp.ones((LEN, 2 * HEAD), BF)
    vx = jnp.concatenate([v_ref[...], ones], axis=1)
    for q0 in range(0, LEN, QB):
        nk = keys_for(q0)
        q = jnp.where(own, q_ref[q0 : q0 + QB, :], jnp.zeros((), BF))
        flat = (q0 // QB) * QB
        parts = []
        if flat:
            parts.append(nt(q, k_ref[0:flat, :]))
        for k0 in range(flat, nk, QB):
            s = nt(q, k_ref[k0 : k0 + QB, :])
            parts.append(jnp.where(allowed(prefix, q0, QB, k0, QB, False), s, MASKED))
        top = parts[0].max(axis=1, keepdims=True)
        for s in parts[1:]:
            top = jnp.maximum(top, s.max(axis=1, keepdims=True))
        probs = [jnp.exp(s - top).astype(BF) for s in parts]
        probs = probs[0] if len(probs) == 1 else jnp.concatenate(probs, axis=1)
        o = nn(probs, vx[0:nk, :])
        total = o[:, 2 * HEAD :]
        ctx = (o[:, : 2 * HEAD] / total).astype(BF)
        half = lax.rem(q0 // HALF_L + ids[1], 2)
        at = pl.ds(q0 % HALF_L, QB)
        c_ref[half, at, :] = jnp.where(own | (h == 0), ctx, c_ref[half, at, :])
        if want_log:
            log_total = top + jnp.log(total)
            rest[0][h, :, q0 : q0 + QB] = jnp.transpose(log_total)[0:8, :]


def attend(at, ids, q, k, v, want_log):
    pair = pl.BlockSpec((LEN, 2 * HEAD), lambda p, ids: (0, at))
    outs = [jax.ShapeDtypeStruct((2, HALF_L, 2 * HEAD), BF)]
    specs = [pl.BlockSpec((2, HALF_L, 2 * HEAD), lambda p, ids: (0, 0, 0))]
    if want_log:
        outs.append(jax.ShapeDtypeStruct((2, 8, LEN), F32))
        specs.append(pl.BlockSpec((2, 8, LEN), lambda p, ids: (0, 0, 0)))
    return pl.pallas_call(
        partial(attend_kernel, want_log),
        out_shape=outs,
        grid_spec=pltpu.PrefetchScalarGridSpec(
            num_scalar_prefetch=1, grid=(2,), in_specs=[pair] * 3, out_specs=specs
        ),
        compiler_params=params(),
        cost_estimate=pl.CostEstimate(
            flops=5 << 30, transcendentals=LEN * LEN, bytes_accessed=2 << 20
        ),
        name="attend",
    )(ids, q, k, v)


def attend_back_kernel(
    ids, q_ref, k_ref, v_ref, c_ref, go_ref, gx_ref, log_ref, gq_ref, gk_ref, gv_ref,
    g_all, mid_all, qt, kacc, vacc
):
    h = lax.rem(pl.program_id(0), 2)
    prefix, t = ids[2], ids[1]
    lane = lax.broadcasted_iota(jnp.int32, (HALF_L, 2 * HEAD), 1)
    own = (lane // HEAD) == h
    zero = jnp.zeros((), BF)
    for half, ref in ((0, go_ref), (1, gx_ref)):
        g = jnp.where(own, ref[...], zero)
        at = pl.ds(pl.multiple_of(lax.rem(t + half, 2) * HALF_L, HALF_L), HALF_L)
        g_all[at, :] = g
        mid = jnp.sum(g.astype(F32) * c_ref[half].astype(F32), axis=1, keepdims=True)
        mid_all[:, at] = jnp.transpose(jnp.broadcast_to(mid, (HALF_L, 2 * HEAD)))[0:8, :]

    @pl.when(h == 0)
    def _():
        qt[...] = jnp.zeros_like(qt)
        kacc[...] = jnp.zeros_like(kacc)
        vacc[...] = jnp.zeros_like(vacc)

    kb = QB
    own_k = (lax.broadcasted_iota(jnp.int32, (kb, 2 * HEAD), 1) // HEAD) == h
    own_q = (lax.broadcasted_iota(jnp.int32, (LEN, 2 * HEAD), 1) // HEAD) == h
    q_all = jnp.where(own_q, q_ref[...], zero)
    for k0 in range(0, LEN, kb):
        k_blk = jnp.where(own_k, k_ref[k0 : k0 + kb, :], zero)
        v_blk = v_ref[k0 : k0 + kb, :]
        q0 = 0 if k0 < PREFIX_MAX else k0
        nq = LEN - q0
        s = nt(k_blk, q_all[q0:, :])
        flat = k0 + kb
        parts = []
        for c0 in range(q0, flat, QB):
            m = allowed(prefix, c0, QB, k0, kb, True)
            parts.append(jnp.where(m, s[:, c0 - q0 : c0 - q0 + QB], MASKED))
        if flat < LEN:
            parts.append(s[:, flat - q0 :])
        s = parts[0] if len(parts) == 1 else jnp.concatenate(parts, axis=1)
        p = jnp.exp(s - log_ref[h, 0:1, q0:])
        g = g_all[q0:, :]
        gp = nt(v_blk, g)
        gs = (p * (gp - mid_all[0:1, q0:])).astype(BF)
        vacc[k0 : k0 + kb, :] += nn(p.astype(BF), g)
        kacc[k0 : k0 + kb, :] += nn(gs, q_all[q0:, :])
        qt[:, q0:] += tn(k_blk, gs)

    @pl.when(h == 1)
    def _():
        gq = jnp.transpose(qt[...]).astype(BF)
        gq_ref[...] = gq * jnp.asarray(1.0 / math.sqrt(HEAD), BF)
        gk_ref[...] = kacc[...].astype(BF)
        gv_ref[...] = vacc[...].astype(BF)


def attend_back(at, ids, q, k, v, ctx, g_own, g_other, logs):
    pair = pl.BlockSpec((LEN, 2 * HEAD), lambda p, ids: (0, at))
    half = pl.BlockSpec((HALF_L, 2 * HEAD), lambda p, ids: (0, at))
    return pl.pallas_call(
        attend_back_kernel,
        out_shape=[jax.ShapeDtypeStruct((LEN, 2 * HEAD), BF)] * 3,
        grid_spec=pltpu.PrefetchScalarGridSpec(
            num_scalar_prefetch=1,
            grid=(2,),
            in_specs=[pair] * 3
            + [pl.BlockSpec((2, HALF_L, 2 * HEAD), lambda p, ids: (0, 0, 0))]
            + [half] * 2
            + [pl.BlockSpec((2, 8, LEN), lambda p, ids: (0, 0, 0))],
            out_specs=[pl.BlockSpec((LEN, 2 * HEAD), lambda p, ids: (0, 0))] * 3,
            scratch_shapes=[
                pltpu.VMEM((LEN, 2 * HEAD), BF),
                pltpu.VMEM((8, LEN), F32),
                pltpu.VMEM((2 * HEAD, LEN), F32),
                pltpu.VMEM((LEN, 2 * HEAD), F32),
                pltpu.VMEM((LEN, 2 * HEAD), F32),
            ],
        ),
        compiler_params=params(),
        cost_estimate=pl.CostEstimate(
            flops=13 << 30, transcendentals=LEN * LEN, bytes_accessed=3 << 20
        ),
        name="attend_back",
    )(ids, q, k, v, ctx, g_own, g_other, logs)


def norm(v):
    centred = v - jnp.mean(v, axis=-1, keepdims=True)
    r = lax.rsqrt(jnp.mean(centred * centred, axis=-1, keepdims=True) + EPS)
    return centred * r, r


def norm_back(g, n, r, gain):
    gn = g * gain
    return r * (
        gn - jnp.mean(gn, axis=-1, keepdims=True) - n * jnp.mean(gn * n, axis=-1, keepdims=True)
    )


INV_ROOT2 = 1.0 / math.sqrt(2.0)
INV_ROOT2PI = 1.0 / math.sqrt(2.0 * math.pi)
FC = 768


def load_layer(ids, np_, rows, own, other, up, down, out, sems):
    if np_ == 1:
        t = ids[1]

        def parts(side):
            return [
                (0, up, side * HALF_F, HALF_F),
                (HALF_F, down, side * HALF_F, HALF_F),
                (2 * HALF_F, out, side * HALF_D, HALF_D),
            ]
    else:
        t = ids[1]
        c = (rows * HALF_D) // (2 * HALF_F + HALF_D)
        f = (rows - c) // 2

        def parts(side):
            return [
                (0, f, up, side * HALF_F),
                (f, f, down, side * HALF_F),
                (2 * f, c, out, side * HALF_D),
            ]

    load_chunks(ids, [(own, t, rows, parts(t)), (other, 1 - t, rows, parts(1 - t))], sems)


def branch(ids, x, c_own, c_other, out, bias):
    c_own = jnp.concatenate([c[0] for c in c_own], axis=1)
    t = ids[1]
    o = nn(c_own, out[rows_at(t * HALF_D, HALF_D), :])
    o = o + nn(c_other, out[rows_at((1 - t) * HALF_D, HALF_D), :])
    return x.astype(F32) + o + bias


def teacher_kernel(np_, rows, ids, x, c0, c1, c2, c_other, row, unit, *rest):
    own, other, rest = rest[:np_], rest[np_ : 2 * np_], rest[2 * np_ :]
    y, up, down, out, sems = rest

    @pl.when(pl.program_id(0) == 0)
    def _():
        load_layer(ids, np_, rows, own, other, up, down, out, sems)

    mixed = branch(ids, x[...], (c0, c1, c2), c_other[...], out, row[0:1, :])
    hidden = norm(mixed)[0] * row[2:3, :] + row[3:4, :]
    hb = hidden.astype(BF)
    total = hidden + row[1:2, :]
    for f in range(0, FF, FC):
        pre = nt(hb, up[f : f + FC, :]) + unit[0:1, f : f + FC]
        act = (pre * (0.5 + 0.5 * lax.erf(pre * INV_ROOT2))).astype(BF)
        total = total + nn(act, down[f : f + FC, :])
    y[...] = norm(total)[0] * row[4:5, :] + row[5:6, :]


def layer_scratch(own, rows):
    n = 2 * count_chunks([(own, rows, 3)])
    return [
        pltpu.VMEM((FF, D), BF),
        pltpu.VMEM((FF, D), BF),
        pltpu.VMEM((D, D), BF),
        pltpu.SemaphoreType.DMA((n,)),
    ]


def block(cols):
    return pl.BlockSpec((TB, cols), lambda i, ids: (i, 0))


def whole(*shape):
    return pl.BlockSpec(shape, lambda i, ids: (0,) * len(shape))


FIRST_HALF = [pl.BlockSpec((1, TB, 2 * HEAD), lambda i, ids: (0, i, 0))] * 3


def teacher_ffn(ids, x, ctx, c_other, row, unit, own, other, rows):
    tokens = x.shape[0]
    np_ = len(own)
    return pl.pallas_call(
        partial(teacher_kernel, np_, rows),
        out_shape=jax.ShapeDtypeStruct((tokens, D), F32),
        grid_spec=pltpu.PrefetchScalarGridSpec(
            num_scalar_prefetch=1,
            grid=(tokens // TB,),
            in_specs=[block(D), *FIRST_HALF, block(HALF_D), whole(6, D), whole(1, FF)]
            + [ANY] * (2 * np_),
            out_specs=block(D),
            scratch_shapes=layer_scratch(own, rows),
        ),
        compiler_params=params(),
        cost_estimate=pl.CostEstimate(
            flops=2 * tokens * D * (2 * FF + D), transcendentals=tokens * FF, bytes_accessed=16 << 20
        ),
        name="teacher_ffn",
    )(ids, x, *ctx, c_other, row, unit, *own, *other)


def student_kernel(np_, rows, ids, x, c0, c1, c2, c_other, y, row, unit, *rest):
    own, other, rest = rest[:np_], rest[np_ : 2 * np_], rest[2 * np_ :]
    (
        student, act_ref, gpre_ref, hid_ref, gffn_ref, gbr_ref, gmix_ref, gown_ref, gother_ref,
        sums, unit_sums, up, down, out, sems, slope
    ) = rest
    i = pl.program_id(0)

    @pl.when(i == 0)
    def _():
        load_layer(ids, np_, rows, own, other, up, down, out, sems)
        sums[...] = jnp.zeros_like(sums)
        unit_sums[...] = jnp.zeros_like(unit_sums)

    mixed = branch(ids, x[...], (c0, c1, c2), c_other[...], out, row[0:1, :])
    n1, r1 = norm(mixed)
    hidden = n1 * row[2:3, :] + row[3:4, :]
    hb = hidden.astype(BF)
    hid_ref[...] = hb
    total = hidden + row[1:2, :]
    for f in range(0, FF, FC):
        pre = nt(hb, up[f : f + FC, :]) + unit[0:1, f : f + FC]
        phi = 0.5 + 0.5 * lax.erf(pre * INV_ROOT2)
        act = (pre * phi).astype(BF)
        slope[:, f : f + FC] = phi + pre * (jnp.exp(pre * pre * -0.5) * INV_ROOT2PI)
        act_ref[:, f : f + FC] = act
        total = total + nn(act, down[f : f + FC, :])
    n2, r2 = norm(total)
    result = n2 * row[4:5, :] + row[5:6, :]
    student[...] = result.astype(BF)
    diff = result - y[...]
    gsum = norm_back(diff, n2, r2, row[4:5, :])
    gffn = gsum.astype(BF)
    gffn_ref[...] = gffn
    ghid = gsum
    for f in range(0, FF, FC):
        gact = nt(gffn, down[f : f + FC, :])
        gpre = (gact * slope[:, f : f + FC]).astype(BF)
        gpre_ref[:, f : f + FC] = gpre
        unit_sums[0:1, f : f + FC] += jnp.sum(gpre.astype(F32), axis=0, keepdims=True)
        ghid = ghid + nn(gpre, up[f : f + FC, :])
    gmix = norm_back(ghid, n1, r1, row[2:3, :])
    gmix_ref[...] = gmix
    gbr = gmix.astype(BF)
    gbr_ref[...] = gbr
    t = ids[1]
    gown_ref[...] = nt(gbr, out[rows_at(t * HALF_D, HALF_D), :]).astype(BF)
    gother_ref[...] = nt(gbr, out[rows_at((1 - t) * HALF_D, HALF_D), :]).astype(BF)
    for j, term in enumerate((gmix, gsum, ghid * n1, ghid, diff * n2, diff)):
        sums[j : j + 1, :] += jnp.sum(term, axis=0, keepdims=True)


def student_ffn(ids, x, ctx, c_other, y, row, unit, own, other, rows):
    tokens = x.shape[0]
    np_ = len(own)
    s = jax.ShapeDtypeStruct
    return pl.pallas_call(
        partial(student_kernel, np_, rows),
        out_shape=[
            s((tokens, D), BF),
            s((tokens, FF), BF),
            s((tokens, FF), BF),
            s((tokens, D), BF),
            s((tokens, D), BF),
            s((tokens, D), BF),
            s((tokens, D), F32),
            s((tokens, HALF_D), BF),
            s((tokens, HALF_D), BF),
            s((8, D), F32),
            s((8, FF), F32),
        ],
        grid_spec=pltpu.PrefetchScalarGridSpec(
            num_scalar_prefetch=1,
            grid=(tokens // TB,),
            in_specs=[block(D), *FIRST_HALF, block(HALF_D), block(D), whole(6, D), whole(1, FF)]
            + [ANY] * (2 * np_),
            out_specs=[
                block(D), block(FF), block(FF), block(D), block(D), block(D), block(D),
                block(HALF_D), block(HALF_D), whole(8, D), whole(8, FF),
            ],
            scratch_shapes=layer_scratch(own, rows) + [pltpu.VMEM((TB, FF), F32)],
        ),
        compiler_params=params(),
        cost_estimate=pl.CostEstimate(
            flops=2 * tokens * D * (4 * FF + 2 * D),
            transcendentals=2 * tokens * FF,
            bytes_accessed=40 << 20,
        ),
        name="student_ffn",
    )(ids, x, *ctx, c_other, y, row, unit, *own, *other)


def store_chunks(ids, side_t, far, rows, outs, off, size, acc, ranks):
    for j, first in ranks:
        k = lax.bitwise_xor(ids[0] // 4, j)
        for p in range(4):
            sub = lax.bitwise_xor(lax.rem(ids[0], 4), piece_mask(p, side_t))
            value = acc[rows_at((first + sub) * size, size), :].astype(BF)
            outs[p // 2][rows_at(((p % 2) * far + k) * rows + off, size), :] = value


def ffn_grad_kernel(flat, far, rows, own_side, ids, act, gpre, hid, gffn, gbr, *rest):
    n_ctx = 3 if own_side else 1
    ctx, outs, acc = rest[:n_ctx], rest[n_ctx:-1], rest[-1]
    i = pl.program_id(0)
    side_t = ids[1] if own_side else 1 - ids[1]
    per = acc.shape[0]

    def context():
        return jnp.concatenate([c[0] for c in ctx], axis=1) if own_side else ctx[0][...]

    if flat:
        up_out, down_out, out_out = outs
        up_out[...] = tn(gpre[...], hid[...])
        down_out[...] = tn(act[...], gffn[...])

        @pl.when(i == 0)
        def _():
            out_out[...] = tn(context(), gbr[...])

        return
    c = (rows * HALF_D) // (2 * HALF_F + HALF_D)
    f = (rows - c) // 2
    groups = per // (4 * f)
    for off, lhs, rhs in ((0, gpre, hid), (f, act, gffn)):
        acc[...] = tn(lhs[...], rhs[...])
        store_chunks(
            ids, side_t, far, rows, outs, off, f, acc,
            [(i * groups + j, 4 * j) for j in range(groups)]
        )

    @pl.when(i == 0)
    def _():
        acc[0:HALF_D, :] = tn(context(), gbr[...])
        store_chunks(
            ids, side_t, far, rows, outs, 2 * f, c, acc, [(j, 4 * j) for j in range(far)]
        )


def ffn_grads(ids, act, gpre, ctx, hid, gffn, gbr, rows, dp, fast, own_side):
    tokens = hid.shape[0]
    far = dp // 4
    fb = HALF_D
    steps = HALF_F // fb

    def col(i, ids):
        side = ids[1] if own_side else 1 - ids[1]
        return (0, side * steps + i)

    if fast:
        out_shape = [jax.ShapeDtypeStruct((2 * far * rows, D), BF)] * 2
        out_specs = [whole(2 * far * rows, D)] * 2
    else:
        out_shape = [
            jax.ShapeDtypeStruct((HALF_F, D), F32),
            jax.ShapeDtypeStruct((HALF_F, D), F32),
            jax.ShapeDtypeStruct((HALF_D, D), F32),
        ]
        cols = pl.BlockSpec((fb, D), lambda i, ids: (i, 0))
        out_specs = [cols, cols, whole(HALF_D, D)]
    return pl.pallas_call(
        partial(ffn_grad_kernel, not fast, far, rows, own_side),
        out_shape=out_shape,
        grid_spec=pltpu.PrefetchScalarGridSpec(
            num_scalar_prefetch=1,
            grid=(steps,),
            in_specs=[
                pl.BlockSpec((tokens, fb), col),
                pl.BlockSpec((tokens, fb), col),
                whole(tokens, D),
                whole(tokens, D),
                whole(tokens, D),
            ]
            + ([whole(1, tokens, 2 * HEAD)] * 3 if own_side else [whole(tokens, HALF_D)]),
            out_specs=out_specs,
            scratch_shapes=[pltpu.VMEM((fb, D), F32)],
        ),
        compiler_params=params(),
        cost_estimate=pl.CostEstimate(
            flops=2 * tokens * D * (FF + HALF_D), transcendentals=0, bytes_accessed=16 << 20
        ),
        name="ffn_grads",
    )(ids, act, gpre, hid, gffn, gbr, *ctx)


def qkv_grad_kernel(flat, far, rows, ids, *rest):
    grads, (x_own, x_other), rest = rest[:9], rest[9:11], rest[11:]
    outs, (x_all, acc) = rest[:-2], rest[-2:]
    i = pl.program_id(0)
    t = ids[1]

    @pl.when(i == 0)
    def _():
        x_all[rows_at(t * HALF_L, HALF_L), :] = x_own[...]
        x_all[rows_at((1 - t) * HALF_L, HALF_L), :] = x_other[...]

    c = rows // 3
    for j in range(3):

        @pl.when(i == j)
        def _():
            g = jnp.concatenate([r[...] for r in grads[j::3]], axis=1)
            value = tn(g, x_all[...])
            if flat:
                outs[0][j * HALF_D : (j + 1) * HALF_D, :] = value
            else:
                acc[...] = value
                store_chunks(
                    ids, t, far, rows, outs, j * c, c, acc, [(r, 4 * r) for r in range(far)]
                )


def qkv_grads(ids, grads, x_own, x_other, rows, dp, fast):
    far = dp // 4
    if fast:
        out_shape = [jax.ShapeDtypeStruct((2 * far * rows, D), BF)] * 2
        out_specs = [whole(2 * far * rows, D)] * 2
    else:
        out_shape = [jax.ShapeDtypeStruct((3 * HALF_D, D), F32)]
        out_specs = [whole(3 * HALF_D, D)]
    return pl.pallas_call(
        partial(qkv_grad_kernel, not fast, far, rows),
        out_shape=out_shape,
        grid_spec=pltpu.PrefetchScalarGridSpec(
            num_scalar_prefetch=1,
            grid=(3,),
            in_specs=[whole(LEN, 2 * HEAD)] * 9 + [whole(HALF_L, D)] * 2,
            out_specs=out_specs,
            scratch_shapes=[pltpu.VMEM((LEN, D), BF), pltpu.VMEM((HALF_D, D), F32)],
        ),
        compiler_params=params(),
        cost_estimate=pl.CostEstimate(
            flops=2 * LEN * 3 * HALF_D * D, transcendentals=0, bytes_accessed=10 << 20
        ),
        name="qkv_grads",
    )(ids, *grads, x_own, x_other)


def binarize(latent, over_axis):
    scale = jnp.mean(jnp.abs(latent), axis=over_axis, keepdims=True)
    return (scale * jnp.sign(latent)).astype(BF)


def local(
    tokens, prefix, qkv_latent, out_latent, up_latent, down_latent, head_bias, up_bias, row_params,
    teacher_qkv, teacher_out, teacher_up, teacher_down, teacher_head_bias, teacher_up_bias,
    teacher_rows,
):
    dp = lax.axis_size("dp")
    n_dev = 2 * dp
    c = qkv_latent.shape[2]
    f = up_latent.shape[1]
    fast = c % 8 == 0 and dp % 4 == 0
    dp_rank = lax.axis_index("dp").astype(jnp.int32)
    t = lax.axis_index("tensor").astype(jnp.int32)
    ids = jnp.stack([dp_rank, t, prefix[0]])

    def qkv_rows(w):
        return jnp.transpose(w, (0, 2, 1)).reshape(3 * c, D)

    def rest_rows(up, down, out):
        return jnp.concatenate([jnp.transpose(up), down, out], axis=0)

    student_a = qkv_rows(binarize(qkv_latent, 1))
    teacher_a = qkv_rows(teacher_qkv)
    student_b = rest_rows(binarize(up_latent, 0), binarize(down_latent, 1), binarize(out_latent, 1))
    teacher_b = rest_rows(teacher_up, teacher_down, teacher_out)

    def small(hb, ub, rp):
        return [hb.reshape(-1), ub, rp.reshape(-1)]

    smalls = jnp.concatenate(
        small(head_bias, up_bias, row_params)
        + small(teacher_head_bias, teacher_up_bias, teacher_rows)
    )
    n_small = smalls.shape[0] // 2
    smalls = lax.all_to_all(jnp.broadcast_to(smalls, (n_dev, 2 * n_small)), BOTH, 0, 0)

    def unpack(part):
        hb = part[:, : 2 * c].reshape(n_dev, 2, c).transpose(1, 0, 2).reshape(2, D)
        ub = part[:, 2 * c : 2 * c + f].reshape(1, FF)
        rp = part[:, 2 * c + f :].reshape(n_dev, 6, c).transpose(1, 0, 2).reshape(6, D)
        return lax.dynamic_slice_in_dim(hb, t * HALF_D, HALF_D, 1), ub, rp

    s_head, s_unit, s_row = unpack(smalls[:, :n_small])
    t_head, t_unit, t_row = unpack(smalls[:, n_small:])

    x_other = swap(tokens, dp)

    def halves(c):
        return jnp.concatenate([p[1] for p in c], axis=1)

    if fast:
        far = dp // 4
        a_rows, b_rows = 3 * c, 2 * f + c

        def steps(n):
            return [1 << i for i in range(n.bit_length() - 1)]

        def far_all(x):
            for k in steps(far)[:-1]:
                x = join(x, far_step(x, dp, k))
            return x

        mine_sa = far_gather(student_a, dp)
        mine_sa, x_other, teacher_a, teacher_b = tie(mine_sa, x_other, teacher_a, teacher_b)
        a_sa = near_a(mine_sa, dp)
        last = far // 2
        ta, tb = far_all(teacher_a), far_all(teacher_b)
        a_sa, ta, tb, s_head = tie(a_sa, ta, tb, s_head)
        both_sa = join(mine_sa, a_sa)
        b_sa = near_b(both_sa, dp)
        ta_in, tb_in = far_step(ta, dp, last), far_step(tb, dp, last)
        b_sa, ta_in = tie(b_sa, ta_in)
        mine_ta = join(ta, ta_in)
        a_ta = near_a(mine_ta, dp)
        pieces_sa = [both_sa, b_sa]
    else:

        def gathered(x, sizes):
            parts, at = [], 0
            for n in sizes:
                parts.append(lax.all_gather(x[at : at + n], "dp", axis=0, tiled=True))
                at += n
            return [jnp.concatenate(parts, axis=0)]

        a_rows, b_rows = 3 * HALF_D, 2 * HALF_F + HALF_D
        pieces_sa = gathered(student_a, (c, c, c))
        pieces_ta = gathered(teacher_a, (c, c, c))
        pieces_tb = gathered(teacher_b, (f, f, c))
        pieces_sb = gathered(student_b, (f, f, c))
        others_tb = [swap(p, dp) for p in pieces_tb]
        others_sb = [swap(p, dp) for p in pieces_sb]

    q, k, v, w_qkv = project(ids, tokens, x_other, s_head, pieces_sa, a_rows)
    if fast:
        q, a_ta, student_b = tie(q, a_ta, student_b)
        both_ta = join(mine_ta, a_ta)
        b_ta = near_b(both_ta, dp)
        sb = far_all(student_b)
    ctx, logs = [None] * 3, [None] * 3
    ctx[0], logs[0] = attend(0, ids, q, k, v, True)
    if fast:
        ctx[0], q, tb_in, sb = tie(ctx[0], q, tb_in, sb)
        mine_tb = join(tb, tb_in)
        a_tb = near_a(mine_tb, dp)
        sb_in = far_step(sb, dp, last)
    ctx[1], logs[1] = attend(1, ids, q, k, v, True)
    ctx[1], q = tie(ctx[1], q)
    ctx[2], logs[2] = attend(2, ids, q, k, v, True)
    if fast:
        ctx[2], a_tb, b_ta = tie(ctx[2], a_tb, b_ta)
        pieces_ta = [both_ta, b_ta]
        both_tb = join(mine_tb, a_tb)
        b_tb = near_b(both_tb, dp)
        others_tb = [swap(both_tb, dp)]
    ctx_other = swap(halves(ctx), dp)
    tq, tk, tv, _ = project(ids, tokens, x_other, t_head, pieces_ta, a_rows)
    if fast:
        tq, sb_in = tie(tq, sb_in)
        mine_sb = join(sb, sb_in)
        a_sb = near_a(mine_sb, dp)
    t_ctx = [None] * 3
    t_ctx[0] = attend(0, ids, tq, tk, tv, False)[0]
    t_ctx[0], tq = tie(t_ctx[0], tq)
    t_ctx[1] = attend(1, ids, tq, tk, tv, False)[0]
    if fast:
        t_ctx[1], tq, b_tb, a_sb, ctx_other = tie(t_ctx[1], tq, b_tb, a_sb, ctx_other)
        pieces_tb = [both_tb, b_tb]
        others_tb.append(swap(b_tb, dp))
        both_sb = join(mine_sb, a_sb)
        b_sb = near_b(both_sb, dp)
        others_sb = [swap(both_sb, dp)]
    t_ctx[2] = attend(2, ids, tq, tk, tv, False)[0]
    t_other = swap(halves(t_ctx), dp)
    y = teacher_ffn(ids, tokens, t_ctx, t_other, t_row, t_unit, pieces_tb, others_tb, b_rows)
    if fast:
        y, b_sb = tie(y, b_sb)
        pieces_sb = [both_sb, b_sb]
        others_sb.append(swap(b_sb, dp))
    (student, act, gpre, hid, gffn, gbr, gmix, g_own, g_send, sums, unit_sums) = student_ffn(
        ids, tokens, ctx, ctx_other, y, s_row, s_unit, pieces_sb, others_sb, b_rows
    )
    g_other = swap(g_send, dp)

    away = ffn_grads(ids, act, gpre, [ctx_other], hid, gffn, gbr, b_rows, dp, fast, False)
    gpre, *away = tie(gpre, *away)
    away = [swap(p, dp) for p in away]
    home = ffn_grads(ids, act, gpre, ctx, hid, gffn, gbr, b_rows, dp, fast, True)

    def back(at):
        return attend_back(at, ids, q, k, v, ctx[at], g_own, g_other, logs[at])

    def near_sum(own, other, received):
        n = own.shape[0] // 2
        terms = (own, *other, received)
        onward = plus(*[x[n:] for x in terms]).astype(BF)
        return [x[:n] for x in terms], near_a(onward, dp)

    if fast:
        away_b = plus(home[1], away[1]).astype(BF)
        g_other, away_b, away[0] = tie(g_other, away_b, away[0])
        b_in = near_b(away_b, dp)
        grads = list(back(0))
        grads[0], k = tie(grads[0], k)
        grads += back(1)
        grads[3], k, b_in = tie(grads[3], k, b_in)
        kept, a_in = near_sum(home[0], [away[0]], b_in)
        grads += back(2)
        grads[6], a_in = tie(grads[6], a_in)
        b_grad = direct_sum(plus(*kept, a_in), dp)
        up_grad, down_grad, out_grad = b_grad[:f], b_grad[f : 2 * f], b_grad[2 * f :]
    else:
        grads = list(back(0)) + list(back(1)) + list(back(2))
        up_grad, down_grad, out_grad = [
            lax.psum_scatter(a + b, "dp", scatter_dimension=0, tiled=True)
            for a, b in zip(home, away)
        ]

    a_pieces = qkv_grads(ids, grads, tokens, x_other, a_rows, dp, fast)
    if fast:
        grads[0], *a_pieces = tie(grads[0], *a_pieces)
        b_in = near_b(a_pieces[1], dp)
        kept, a_in = near_sum(a_pieces[0], [], b_in)
        qkv_grad = direct_sum(plus(*kept, a_in), dp).reshape(3, c, D)
    else:
        qkv_grad = lax.psum_scatter(
            a_pieces[0].reshape(3, HALF_D, D), "dp", scatter_dimension=1, tiled=True
        )

    gq, gk, gv = [jnp.concatenate(grads[j::3], axis=1) for j in range(3)]
    back_rows = jnp.concatenate([gq, gk, gv], axis=1)
    theirs = lax.dynamic_slice_in_dim(back_rows, (1 - t) * HALF_L, HALF_L, 0)
    ours = lax.dynamic_slice_in_dim(back_rows, t * HALF_L, HALF_L, 0)
    back_other = swap(nn(theirs, w_qkv).astype(BF), dp)
    token_grad = gmix + nn(ours, w_qkv) + back_other.astype(F32)

    head_sums = jnp.stack(
        [jnp.sum(gq.astype(F32), axis=0), jnp.sum(gv.astype(F32), axis=0)]
    )
    head_sums = lax.dynamic_update_slice_in_dim(
        jnp.zeros((2, D), F32), head_sums, t * HALF_D, 1
    )
    small_grads = jnp.concatenate(
        [
            head_sums.reshape(2, n_dev, c).transpose(1, 0, 2).reshape(n_dev, 2 * c),
            unit_sums[0].reshape(n_dev, f),
            sums[:6].reshape(6, n_dev, c).transpose(1, 0, 2).reshape(n_dev, 6 * c),
        ],
        axis=1,
    )
    small_grads = jnp.sum(lax.all_to_all(small_grads, BOTH, 0, 0), axis=0)

    return (
        student,
        token_grad,
        jnp.transpose(qkv_grad, (0, 2, 1)),
        out_grad,
        jnp.transpose(up_grad),
        down_grad,
        small_grads[: 2 * c].reshape(2, c),
        small_grads[2 * c : 2 * c + f],
        small_grads[2 * c + f :].reshape(6, c),
    )


def solution(mesh):
    both, weight = ("dp", "tensor"), ("tensor", "dp")
    params_spec = (
        P(None, None, weight),
        P(weight, None),
        P(None, weight),
        P(weight, None),
        P(None, both),
        P(both),
        P(None, both),
    )
    return jax.shard_map(
        local,
        mesh=mesh,
        in_specs=(P(both, None), P("dp")) + params_spec + params_spec,
        out_specs=(P(both, None), P(both, None)) + params_spec,
        check_vma=False,
    )
```

```python
import math
from functools import partial

import jax
import jax.numpy as jnp
from jax import lax
from jax.experimental import pallas as pl
from jax.experimental.pallas import tpu as pltpu
from jax.sharding import PartitionSpec as P

D = 768
FF = 3072
HEAD = 64
LEN = 2048
HALF_D = D // 2
HALF_F = FF // 2
HALF_L = LEN // 2
PREFIX_MAX = LEN // 2
QB = 256
TB = 256
EPS = 1e-05
MASKED = -1e30
BF = jnp.bfloat16
F32 = jnp.float32
BOTH = ("dp", "tensor")
VMEM_LIMIT = 60 * 1024 * 1024


def nt(a, b):
    return lax.dot_general(a, b, (((1,), (1,)), ((), ())), preferred_element_type=F32)


def nn(a, b):
    return lax.dot_general(a, b, (((1,), (0,)), ((), ())), preferred_element_type=F32)


def tn(a, b):
    return lax.dot_general(a, b, (((0,), (0,)), ((), ())), preferred_element_type=F32)


def swap_route(dp):
    return [(2 * d + t, 2 * d + 1 - t) for d in range(dp) for t in range(2)]


def far_route(dp, k):
    return [(2 * d + t, 2 * (d ^ (4 * k)) + t) for d in range(dp) for t in range(2)]


def near_route(dp, which):
    out = []
    for d in range(dp):
        for t in range(2):
            bit = 2 if (t == 0) == (which == 0) else 1
            out.append((2 * d + t, 2 * (d ^ bit) + t))
    return out


def send(x, route):
    return lax.ppermute(x, BOTH, route)


def far_gather(chunk, dp):
    return jnp.concatenate(
        [chunk] + [send(chunk, far_route(dp, k)) for k in range(1, dp // 4)], axis=0
    )


def far_step(x, dp, k):
    return send(x, far_route(dp, k))


def join(a, b):
    return jnp.concatenate([a, b], axis=0)


def near_a(x, dp):
    return send(x, near_route(dp, 0))


def near_b(x, dp):
    return send(x, near_route(dp, 1))


def swap(x, dp):
    return send(x, swap_route(dp))


def plus(*xs):
    out = xs[0].astype(F32)
    for x in xs[1:]:
        out = out + x.astype(F32)
    return out


def direct_sum(total, dp):
    far = dp // 4
    rows = total.shape[0] // far
    parts = [total[k * rows : (k + 1) * rows] for k in range(far)]
    return plus(
        parts[0], *[far_step(parts[k].astype(BF), dp, k) for k in range(1, far)]
    )


def tie(*xs):
    return lax.optimization_barrier(xs)


def piece_mask(p, t):
    if p == 0:
        return 0
    if p == 3:
        return 3
    return jnp.where((t == 0) == (p == 1), 2, 1)


def rank_of(ids, t, p, k):
    return lax.bitwise_xor(ids[0], 4 * k + piece_mask(p, t))


def rows_at(start, size):
    return pl.ds(pl.multiple_of(start, 8), size)


def load_chunks(ids, sets, sems):
    copies = []
    for pieces, t, rows, parts in sets:
        if len(pieces) == 1:
            for src, target, base, size in parts:
                copies.append((pieces[0].at[pl.ds(src, size)], target.at[rows_at(base, size)]))
            continue
        for p, piece in enumerate(pieces):
            far = piece.shape[0] // rows // 2
            for k in range(2 * far):
                r = rank_of(ids, t, 2 * p + k // far, k % far)
                for off, size, target, base in parts:
                    copies.append(
                        (
                            piece.at[pl.ds(k * rows + off, size)],
                            target.at[rows_at(base + r * size, size)],
                        )
                    )
    copies = [pltpu.make_async_copy(s, d, sems.at[i]) for i, (s, d) in enumerate(copies)]
    for c in copies:
        c.start()
    for c in copies:
        c.wait()


def count_chunks(sets):
    n = 0
    for pieces, rows, parts in sets:
        n += parts if len(pieces) == 1 else parts * sum(p.shape[0] // rows for p in pieces)
    return n


ANY = pl.BlockSpec(memory_space=pl.ANY)
COST_SHARE = 16


def cost(flops, exps, moved):
    return pl.CostEstimate(
        flops=flops // COST_SHARE,
        transcendentals=exps // COST_SHARE,
        bytes_accessed=moved // COST_SHARE,
    )


def params(n=1):
    return pltpu.CompilerParams(
        dimension_semantics=("arbitrary",) * n, vmem_limit_bytes=VMEM_LIMIT
    )


def qkv_kernel(np_, rows, ids, x_own, x_other, bias, *rest):
    pieces, rest = rest[:np_], rest[np_:]
    q_ref, k_ref, v_ref, w, sems = rest
    i = pl.program_id(0)
    c = rows // 3

    @pl.when(i == 0)
    def _():
        if np_ == 1:
            parts = [(0, w, 0, 3 * HALF_D)]
        else:
            parts = [(j * c, c, w, j * HALF_D) for j in range(3)]
        load_chunks(ids, [(pieces, ids[1], rows, parts)], sems)

    x = jnp.where(i // 2 == ids[1], x_own[...], x_other[...])
    q_ref[...] = ((nt(x, w[0:HALF_D, :]) + bias[0:1, :]) * (1.0 / math.sqrt(HEAD))).astype(BF)
    k_ref[...] = nt(x, w[HALF_D : 2 * HALF_D, :]).astype(BF)
    v_ref[...] = (nt(x, w[2 * HALF_D :, :]) + bias[1:2, :]).astype(BF)


def project(ids, x_own, x_other, bias, pieces, rows):
    tb = 512
    np_ = len(pieces)
    n = count_chunks([(pieces, rows, 1 if np_ == 1 else 3)])
    xs = pl.BlockSpec((tb, D), lambda i, ids: (i % 2, 0))
    full = pl.BlockSpec((tb, HALF_D), lambda i, ids: (i, 0))
    return pl.pallas_call(
        partial(qkv_kernel, np_, rows),
        out_shape=[jax.ShapeDtypeStruct((LEN, HALF_D), BF)] * 3
        + [jax.ShapeDtypeStruct((3 * HALF_D, D), BF)],
        grid_spec=pltpu.PrefetchScalarGridSpec(
            num_scalar_prefetch=1,
            grid=(LEN // tb,),
            in_specs=[xs, xs, pl.BlockSpec((2, HALF_D), lambda i, ids: (0, 0))] + [ANY] * np_,
            out_specs=[full] * 3 + [pl.BlockSpec((3 * HALF_D, D), lambda i, ids: (0, 0))],
            scratch_shapes=[pltpu.SemaphoreType.DMA((n,))],
        ),
        compiler_params=params(),
        cost_estimate=cost(2 * LEN * 3 * HALF_D * D, 0, 12 << 20),
        name="project",
    )(ids, x_own, x_other, bias, *pieces)


def allowed(prefix, q0, nq, k0, nk, keys_first):
    if k0 + nk - 1 <= q0:
        return None
    shape, ka, qa = ((nk, nq), 0, 1) if keys_first else ((nq, nk), 1, 0)
    kp = k0 + lax.broadcasted_iota(jnp.int32, shape, ka)
    qp = q0 + lax.broadcasted_iota(jnp.int32, shape, qa)
    causal = kp <= qp
    if k0 >= PREFIX_MAX:
        return causal
    if k0 > q0 + nq - 1:
        return kp < prefix
    return causal | (kp < prefix)


def keys_for(q0):
    return max(q0 + QB, PREFIX_MAX)


def attend_kernel(want_log, ids, q_ref, k_ref, v_ref, c_ref, *rest):
    h = lax.rem(pl.program_id(0), 2)
    prefix = ids[2]
    lane = lax.broadcasted_iota(jnp.int32, (QB, 2 * HEAD), 1)
    own = (lane // HEAD) == h
    ones = jnp.ones((LEN, 2 * HEAD), BF)
    vx = jnp.concatenate([v_ref[...], ones], axis=1)
    for q0 in range(0, LEN, QB):
        nk = keys_for(q0)
        q = jnp.where(own, q_ref[q0 : q0 + QB, :], jnp.zeros((), BF))
        flat = (q0 // QB) * QB
        parts = []
        if flat:
            parts.append(nt(q, k_ref[0:flat, :]))
        for k0 in range(flat, nk, QB):
            s = nt(q, k_ref[k0 : k0 + QB, :])
            parts.append(jnp.where(allowed(prefix, q0, QB, k0, QB, False), s, MASKED))
        top = parts[0].max(axis=1, keepdims=True)
        for s in parts[1:]:
            top = jnp.maximum(top, s.max(axis=1, keepdims=True))
        probs = [jnp.exp(s - top).astype(BF) for s in parts]
        probs = probs[0] if len(probs) == 1 else jnp.concatenate(probs, axis=1)
        o = nn(probs, vx[0:nk, :])
        total = o[:, 2 * HEAD :]
        ctx = (o[:, : 2 * HEAD] / total).astype(BF)
        half = lax.rem(q0 // HALF_L + ids[1], 2)
        at = pl.ds(q0 % HALF_L, QB)
        c_ref[half, at, :] = jnp.where(own | (h == 0), ctx, c_ref[half, at, :])
        if want_log:
            log_total = top + jnp.log(total)
            rest[0][h, :, q0 : q0 + QB] = jnp.transpose(log_total)[0:8, :]


def attend(at, n, ids, q, k, v, want_log):
    pair = pl.BlockSpec((LEN, 2 * HEAD), lambda p, ids: (0, at + p // 2))
    outs = [jax.ShapeDtypeStruct((2, HALF_L, n * 2 * HEAD), BF)]
    specs = [pl.BlockSpec((2, HALF_L, 2 * HEAD), lambda p, ids: (0, 0, p // 2))]
    if want_log:
        outs.append(jax.ShapeDtypeStruct((2 * n, 8, LEN), F32))
        specs.append(pl.BlockSpec((2, 8, LEN), lambda p, ids: (p // 2, 0, 0)))
    return pl.pallas_call(
        partial(attend_kernel, want_log),
        out_shape=outs,
        grid_spec=pltpu.PrefetchScalarGridSpec(
            num_scalar_prefetch=1, grid=(2 * n,), in_specs=[pair] * 3, out_specs=specs
        ),
        compiler_params=params(),
        cost_estimate=cost(n * (5 << 30), n * LEN * LEN, n << 21),
        name="attend",
    )(ids, q, k, v)


def attend_back_kernel(
    ids, q_ref, k_ref, v_ref, c_ref, go_ref, gx_ref, log_ref, gq_ref, gk_ref, gv_ref,
    g_all, mid_all, qt, kacc, vacc
):
    h = lax.rem(pl.program_id(0), 2)
    prefix, t = ids[2], ids[1]
    lane = lax.broadcasted_iota(jnp.int32, (HALF_L, 2 * HEAD), 1)
    own = (lane // HEAD) == h
    zero = jnp.zeros((), BF)
    for half, ref in ((0, go_ref), (1, gx_ref)):
        g = jnp.where(own, ref[...], zero)
        at = pl.ds(pl.multiple_of(lax.rem(t + half, 2) * HALF_L, HALF_L), HALF_L)
        g_all[at, :] = g
        mid = jnp.sum(g.astype(F32) * c_ref[half].astype(F32), axis=1, keepdims=True)
        mid_all[:, at] = jnp.transpose(jnp.broadcast_to(mid, (HALF_L, 2 * HEAD)))[0:8, :]

    @pl.when(h == 0)
    def _():
        qt[...] = jnp.zeros_like(qt)
        kacc[...] = jnp.zeros_like(kacc)
        vacc[...] = jnp.zeros_like(vacc)

    kb = QB
    own_k = (lax.broadcasted_iota(jnp.int32, (kb, 2 * HEAD), 1) // HEAD) == h
    own_q = (lax.broadcasted_iota(jnp.int32, (LEN, 2 * HEAD), 1) // HEAD) == h
    q_all = jnp.where(own_q, q_ref[...], zero)
    for k0 in range(0, LEN, kb):
        k_blk = jnp.where(own_k, k_ref[k0 : k0 + kb, :], zero)
        v_blk = v_ref[k0 : k0 + kb, :]
        q0 = 0 if k0 < PREFIX_MAX else k0
        nq = LEN - q0
        s = nt(k_blk, q_all[q0:, :])
        flat = k0 + kb
        parts = []
        for c0 in range(q0, flat, QB):
            m = allowed(prefix, c0, QB, k0, kb, True)
            parts.append(jnp.where(m, s[:, c0 - q0 : c0 - q0 + QB], MASKED))
        if flat < LEN:
            parts.append(s[:, flat - q0 :])
        s = parts[0] if len(parts) == 1 else jnp.concatenate(parts, axis=1)
        p = jnp.exp(s - log_ref[h, 0:1, q0:])
        g = g_all[q0:, :]
        gp = nt(v_blk, g)
        gs = (p * (gp - mid_all[0:1, q0:])).astype(BF)
        vacc[k0 : k0 + kb, :] += nn(p.astype(BF), g)
        kacc[k0 : k0 + kb, :] += nn(gs, q_all[q0:, :])
        qt[:, q0:] += tn(k_blk, gs)

    @pl.when(h == 1)
    def _():
        gq = jnp.transpose(qt[...]).astype(BF)
        gq_ref[...] = gq * jnp.asarray(1.0 / math.sqrt(HEAD), BF)
        gk_ref[...] = kacc[...].astype(BF)
        gv_ref[...] = vacc[...].astype(BF)


def attend_back(at, n, ids, q, k, v, ctx, g_own, g_other, logs):
    pair = pl.BlockSpec((LEN, 2 * HEAD), lambda p, ids: (0, at + p // 2))
    half = pl.BlockSpec((HALF_L, 2 * HEAD), lambda p, ids: (0, at + p // 2))
    return pl.pallas_call(
        attend_back_kernel,
        out_shape=[jax.ShapeDtypeStruct((LEN, n * 2 * HEAD), BF)] * 3,
        grid_spec=pltpu.PrefetchScalarGridSpec(
            num_scalar_prefetch=1,
            grid=(2 * n,),
            in_specs=[pair] * 3
            + [pl.BlockSpec((2, HALF_L, 2 * HEAD), lambda p, ids: (0, 0, at + p // 2))]
            + [half] * 2
            + [pl.BlockSpec((2, 8, LEN), lambda p, ids: (at + p // 2, 0, 0))],
            out_specs=[pl.BlockSpec((LEN, 2 * HEAD), lambda p, ids: (0, p // 2))] * 3,
            scratch_shapes=[
                pltpu.VMEM((LEN, 2 * HEAD), BF),
                pltpu.VMEM((8, LEN), F32),
                pltpu.VMEM((2 * HEAD, LEN), F32),
                pltpu.VMEM((LEN, 2 * HEAD), F32),
                pltpu.VMEM((LEN, 2 * HEAD), F32),
            ],
        ),
        compiler_params=params(),
        cost_estimate=cost(n * (13 << 30), n * LEN * LEN, n * (3 << 20)),
        name="attend_back",
    )(ids, q, k, v, ctx, g_own, g_other, logs)


def norm(v):
    centred = v - jnp.mean(v, axis=-1, keepdims=True)
    r = lax.rsqrt(jnp.mean(centred * centred, axis=-1, keepdims=True) + EPS)
    return centred * r, r


def norm_back(g, n, r, gain):
    gn = g * gain
    return r * (
        gn - jnp.mean(gn, axis=-1, keepdims=True) - n * jnp.mean(gn * n, axis=-1, keepdims=True)
    )


INV_ROOT2 = 1.0 / math.sqrt(2.0)
INV_ROOT2PI = 1.0 / math.sqrt(2.0 * math.pi)
FC = 768


def load_layer(ids, np_, rows, own, other, up, down, out, sems):
    if np_ == 1:
        t = ids[1]

        def parts(side):
            return [
                (0, up, side * HALF_F, HALF_F),
                (HALF_F, down, side * HALF_F, HALF_F),
                (2 * HALF_F, out, side * HALF_D, HALF_D),
            ]
    else:
        t = ids[1]
        c = (rows * HALF_D) // (2 * HALF_F + HALF_D)
        f = (rows - c) // 2

        def parts(side):
            return [
                (0, f, up, side * HALF_F),
                (f, f, down, side * HALF_F),
                (2 * f, c, out, side * HALF_D),
            ]

    load_chunks(ids, [(own, t, rows, parts(t)), (other, 1 - t, rows, parts(1 - t))], sems)


def branch(ids, x, c_own, c_other, out, bias):
    c_own = jnp.concatenate([c[0] for c in c_own], axis=1)
    t = ids[1]
    o = nn(c_own, out[rows_at(t * HALF_D, HALF_D), :])
    o = o + nn(c_other, out[rows_at((1 - t) * HALF_D, HALF_D), :])
    return x.astype(F32) + o + bias


def teacher_kernel(np_, rows, ids, x, c0, c1, c_other, row, unit, *rest):
    own, other, rest = rest[:np_], rest[np_ : 2 * np_], rest[2 * np_ :]
    y, up, down, out, sems = rest

    @pl.when(pl.program_id(0) == 0)
    def _():
        load_layer(ids, np_, rows, own, other, up, down, out, sems)

    mixed = branch(ids, x[...], (c0, c1), c_other[...], out, row[0:1, :])
    hidden = norm(mixed)[0] * row[2:3, :] + row[3:4, :]
    hb = hidden.astype(BF)
    total = hidden + row[1:2, :]
    for f in range(0, FF, FC):
        pre = nt(hb, up[f : f + FC, :]) + unit[0:1, f : f + FC]
        act = (pre * (0.5 + 0.5 * lax.erf(pre * INV_ROOT2))).astype(BF)
        total = total + nn(act, down[f : f + FC, :])
    y[...] = norm(total)[0] * row[4:5, :] + row[5:6, :]


def layer_scratch(own, rows):
    n = 2 * count_chunks([(own, rows, 3)])
    return [
        pltpu.VMEM((FF, D), BF),
        pltpu.VMEM((FF, D), BF),
        pltpu.VMEM((D, D), BF),
        pltpu.SemaphoreType.DMA((n,)),
    ]


def block(cols):
    return pl.BlockSpec((TB, cols), lambda i, ids: (i, 0))


def whole(*shape):
    return pl.BlockSpec(shape, lambda i, ids: (0,) * len(shape))


def own_half(ctx):
    return [pl.BlockSpec((1, TB, c.shape[2]), lambda i, ids: (0, i, 0)) for c in ctx]


def teacher_ffn(ids, x, ctx, c_other, row, unit, own, other, rows):
    tokens = x.shape[0]
    np_ = len(own)
    return pl.pallas_call(
        partial(teacher_kernel, np_, rows),
        out_shape=jax.ShapeDtypeStruct((tokens, D), F32),
        grid_spec=pltpu.PrefetchScalarGridSpec(
            num_scalar_prefetch=1,
            grid=(tokens // TB,),
            in_specs=[block(D), *own_half(ctx), block(HALF_D), whole(6, D), whole(1, FF)]
            + [ANY] * (2 * np_),
            out_specs=block(D),
            scratch_shapes=layer_scratch(own, rows),
        ),
        compiler_params=params(),
        cost_estimate=cost(2 * tokens * D * (2 * FF + D), tokens * FF, 16 << 20),
        name="teacher_ffn",
    )(ids, x, *ctx, c_other, row, unit, *own, *other)


def student_kernel(np_, rows, ids, x, c0, c1, c_other, y, row, unit, *rest):
    own, other, rest = rest[:np_], rest[np_ : 2 * np_], rest[2 * np_ :]
    (
        student, act_ref, gpre_ref, hid_ref, gffn_ref, gbr_ref, gmix_ref, gown_ref, gother_ref,
        sums, unit_sums, up, down, out, sems, slope
    ) = rest
    i = pl.program_id(0)

    @pl.when(i == 0)
    def _():
        load_layer(ids, np_, rows, own, other, up, down, out, sems)
        sums[...] = jnp.zeros_like(sums)
        unit_sums[...] = jnp.zeros_like(unit_sums)

    mixed = branch(ids, x[...], (c0, c1), c_other[...], out, row[0:1, :])
    n1, r1 = norm(mixed)
    hidden = n1 * row[2:3, :] + row[3:4, :]
    hb = hidden.astype(BF)
    hid_ref[...] = hb
    total = hidden + row[1:2, :]
    for f in range(0, FF, FC):
        pre = nt(hb, up[f : f + FC, :]) + unit[0:1, f : f + FC]
        phi = 0.5 + 0.5 * lax.erf(pre * INV_ROOT2)
        act = (pre * phi).astype(BF)
        slope[:, f : f + FC] = phi + pre * (jnp.exp(pre * pre * -0.5) * INV_ROOT2PI)
        act_ref[:, f : f + FC] = act
        total = total + nn(act, down[f : f + FC, :])
    n2, r2 = norm(total)
    result = n2 * row[4:5, :] + row[5:6, :]
    student[...] = result.astype(BF)
    diff = result - y[...]
    gsum = norm_back(diff, n2, r2, row[4:5, :])
    gffn = gsum.astype(BF)
    gffn_ref[...] = gffn
    ghid = gsum
    for f in range(0, FF, FC):
        gact = nt(gffn, down[f : f + FC, :])
        gpre = (gact * slope[:, f : f + FC]).astype(BF)
        gpre_ref[:, f : f + FC] = gpre
        unit_sums[0:1, f : f + FC] += jnp.sum(gpre.astype(F32), axis=0, keepdims=True)
        ghid = ghid + nn(gpre, up[f : f + FC, :])
    gmix = norm_back(ghid, n1, r1, row[2:3, :])
    gmix_ref[...] = gmix
    gbr = gmix.astype(BF)
    gbr_ref[...] = gbr
    t = ids[1]
    gown_ref[...] = nt(gbr, out[rows_at(t * HALF_D, HALF_D), :]).astype(BF)
    gother_ref[...] = nt(gbr, out[rows_at((1 - t) * HALF_D, HALF_D), :]).astype(BF)
    for j, term in enumerate((gmix, gsum, ghid * n1, ghid, diff * n2, diff)):
        sums[j : j + 1, :] += jnp.sum(term, axis=0, keepdims=True)


def student_ffn(ids, x, ctx, c_other, y, row, unit, own, other, rows):
    tokens = x.shape[0]
    np_ = len(own)
    s = jax.ShapeDtypeStruct
    return pl.pallas_call(
        partial(student_kernel, np_, rows),
        out_shape=[
            s((tokens, D), BF),
            s((tokens, FF), BF),
            s((tokens, FF), BF),
            s((tokens, D), BF),
            s((tokens, D), BF),
            s((tokens, D), BF),
            s((tokens, D), F32),
            s((tokens, HALF_D), BF),
            s((tokens, HALF_D), BF),
            s((8, D), F32),
            s((8, FF), F32),
        ],
        grid_spec=pltpu.PrefetchScalarGridSpec(
            num_scalar_prefetch=1,
            grid=(tokens // TB,),
            in_specs=[block(D), *own_half(ctx), block(HALF_D), block(D), whole(6, D), whole(1, FF)]
            + [ANY] * (2 * np_),
            out_specs=[
                block(D), block(FF), block(FF), block(D), block(D), block(D), block(D),
                block(HALF_D), block(HALF_D), whole(8, D), whole(8, FF),
            ],
            scratch_shapes=layer_scratch(own, rows) + [pltpu.VMEM((TB, FF), F32)],
        ),
        compiler_params=params(),
        cost_estimate=cost(2 * tokens * D * (4 * FF + 2 * D), 2 * tokens * FF, 40 << 20),
        name="student_ffn",
    )(ids, x, *ctx, c_other, y, row, unit, *own, *other)


def store_chunks(ids, side_t, far, rows, outs, off, size, acc, ranks):
    for j, first in ranks:
        k = lax.bitwise_xor(ids[0] // 4, j)
        for p in range(4):
            sub = lax.bitwise_xor(lax.rem(ids[0], 4), piece_mask(p, side_t))
            value = acc[rows_at((first + sub) * size, size), :].astype(BF)
            outs[p // 2][rows_at(((p % 2) * far + k) * rows + off, size), :] = value


def ffn_grad_kernel(flat, far, rows, own_side, ids, act, gpre, hid, gffn, gbr, *rest):
    n_ctx = 2 if own_side else 1
    ctx, outs, acc = rest[:n_ctx], rest[n_ctx:-1], rest[-1]
    i = pl.program_id(0)
    side_t = ids[1] if own_side else 1 - ids[1]
    per = acc.shape[0]

    def context():
        return jnp.concatenate([c[0] for c in ctx], axis=1) if own_side else ctx[0][...]

    if flat:
        up_out, down_out, out_out = outs
        up_out[...] = tn(gpre[...], hid[...])
        down_out[...] = tn(act[...], gffn[...])

        @pl.when(i == 0)
        def _():
            out_out[...] = tn(context(), gbr[...])

        return
    c = (rows * HALF_D) // (2 * HALF_F + HALF_D)
    f = (rows - c) // 2
    groups = per // (4 * f)
    for off, lhs, rhs in ((0, gpre, hid), (f, act, gffn)):
        acc[...] = tn(lhs[...], rhs[...])
        store_chunks(
            ids, side_t, far, rows, outs, off, f, acc,
            [(i * groups + j, 4 * j) for j in range(groups)]
        )

    @pl.when(i == 0)
    def _():
        acc[0:HALF_D, :] = tn(context(), gbr[...])
        store_chunks(
            ids, side_t, far, rows, outs, 2 * f, c, acc, [(j, 4 * j) for j in range(far)]
        )


def ffn_grads(ids, act, gpre, ctx, hid, gffn, gbr, rows, dp, fast, own_side):
    tokens = hid.shape[0]
    far = dp // 4
    fb = HALF_D
    steps = HALF_F // fb

    def col(i, ids):
        side = ids[1] if own_side else 1 - ids[1]
        return (0, side * steps + i)

    if fast:
        out_shape = [jax.ShapeDtypeStruct((2 * far * rows, D), BF)] * 2
        out_specs = [whole(2 * far * rows, D)] * 2
    else:
        out_shape = [
            jax.ShapeDtypeStruct((HALF_F, D), F32),
            jax.ShapeDtypeStruct((HALF_F, D), F32),
            jax.ShapeDtypeStruct((HALF_D, D), F32),
        ]
        cols = pl.BlockSpec((fb, D), lambda i, ids: (i, 0))
        out_specs = [cols, cols, whole(HALF_D, D)]
    return pl.pallas_call(
        partial(ffn_grad_kernel, not fast, far, rows, own_side),
        out_shape=out_shape,
        grid_spec=pltpu.PrefetchScalarGridSpec(
            num_scalar_prefetch=1,
            grid=(steps,),
            in_specs=[
                pl.BlockSpec((tokens, fb), col),
                pl.BlockSpec((tokens, fb), col),
                whole(tokens, D),
                whole(tokens, D),
                whole(tokens, D),
            ]
            + [whole(*((1,) if own_side else ()), *c.shape[own_side:]) for c in ctx],
            out_specs=out_specs,
            scratch_shapes=[pltpu.VMEM((fb, D), F32)],
        ),
        compiler_params=params(),
        cost_estimate=cost(2 * tokens * D * (FF + HALF_D), 0, 16 << 20),
        name="ffn_grads",
    )(ids, act, gpre, hid, gffn, gbr, *ctx)


def qkv_grad_kernel(flat, far, rows, ids, *rest):
    grads, (x_own, x_other), rest = rest[:6], rest[6:8], rest[8:]
    outs, (x_all, acc) = rest[:-2], rest[-2:]
    i = pl.program_id(0)
    t = ids[1]

    @pl.when(i == 0)
    def _():
        x_all[rows_at(t * HALF_L, HALF_L), :] = x_own[...]
        x_all[rows_at((1 - t) * HALF_L, HALF_L), :] = x_other[...]

    c = rows // 3
    for j in range(3):

        @pl.when(i == j)
        def _():
            g = jnp.concatenate([r[...] for r in grads[j::3]], axis=1)
            value = tn(g, x_all[...])
            if flat:
                outs[0][j * HALF_D : (j + 1) * HALF_D, :] = value
            else:
                acc[...] = value
                store_chunks(
                    ids, t, far, rows, outs, j * c, c, acc, [(r, 4 * r) for r in range(far)]
                )


def qkv_grads(ids, grads, x_own, x_other, rows, dp, fast):
    far = dp // 4
    if fast:
        out_shape = [jax.ShapeDtypeStruct((2 * far * rows, D), BF)] * 2
        out_specs = [whole(2 * far * rows, D)] * 2
    else:
        out_shape = [jax.ShapeDtypeStruct((3 * HALF_D, D), F32)]
        out_specs = [whole(3 * HALF_D, D)]
    return pl.pallas_call(
        partial(qkv_grad_kernel, not fast, far, rows),
        out_shape=out_shape,
        grid_spec=pltpu.PrefetchScalarGridSpec(
            num_scalar_prefetch=1,
            grid=(3,),
            in_specs=[whole(*g.shape) for g in grads] + [whole(HALF_L, D)] * 2,
            out_specs=out_specs,
            scratch_shapes=[pltpu.VMEM((LEN, D), BF), pltpu.VMEM((HALF_D, D), F32)],
        ),
        compiler_params=params(),
        cost_estimate=cost(2 * LEN * 3 * HALF_D * D, 0, 10 << 20),
        name="qkv_grads",
    )(ids, *grads, x_own, x_other)


def binarize(latent, over_axis):
    scale = jnp.mean(jnp.abs(latent), axis=over_axis, keepdims=True)
    return (scale * jnp.sign(latent)).astype(BF)


def local(
    tokens, prefix, qkv_latent, out_latent, up_latent, down_latent, head_bias, up_bias, row_params,
    teacher_qkv, teacher_out, teacher_up, teacher_down, teacher_head_bias, teacher_up_bias,
    teacher_rows,
):
    dp = lax.axis_size("dp")
    n_dev = 2 * dp
    c = qkv_latent.shape[2]
    f = up_latent.shape[1]
    fast = c % 8 == 0 and dp % 4 == 0
    dp_rank = lax.axis_index("dp").astype(jnp.int32)
    t = lax.axis_index("tensor").astype(jnp.int32)
    ids = jnp.stack([dp_rank, t, prefix[0]])

    def qkv_rows(w):
        return jnp.transpose(w, (0, 2, 1)).reshape(3 * c, D)

    def rest_rows(up, down, out):
        return jnp.concatenate([jnp.transpose(up), down, out], axis=0)

    student_a = qkv_rows(binarize(qkv_latent, 1))
    teacher_a = qkv_rows(teacher_qkv)
    student_b = rest_rows(binarize(up_latent, 0), binarize(down_latent, 1), binarize(out_latent, 1))
    teacher_b = rest_rows(teacher_up, teacher_down, teacher_out)

    def small(hb, ub, rp):
        return [hb.reshape(-1), ub, rp.reshape(-1)]

    smalls = jnp.concatenate(
        small(head_bias, up_bias, row_params)
        + small(teacher_head_bias, teacher_up_bias, teacher_rows)
    )
    n_small = smalls.shape[0] // 2
    smalls = lax.all_to_all(jnp.broadcast_to(smalls, (n_dev, 2 * n_small)), BOTH, 0, 0)

    def unpack(part):
        hb = part[:, : 2 * c].reshape(n_dev, 2, c).transpose(1, 0, 2).reshape(2, D)
        ub = part[:, 2 * c : 2 * c + f].reshape(1, FF)
        rp = part[:, 2 * c + f :].reshape(n_dev, 6, c).transpose(1, 0, 2).reshape(6, D)
        return lax.dynamic_slice_in_dim(hb, t * HALF_D, HALF_D, 1), ub, rp

    s_head, s_unit, s_row = unpack(smalls[:, :n_small])
    t_head, t_unit, t_row = unpack(smalls[:, n_small:])

    x_other = swap(tokens, dp)

    def halves(c):
        return jnp.concatenate([p[1] for p in c], axis=1)

    if fast:
        far = dp // 4
        a_rows, b_rows = 3 * c, 2 * f + c

        def steps(n):
            return [1 << i for i in range(n.bit_length() - 1)]

        def far_all(x):
            for k in steps(far)[:-1]:
                x = join(x, far_step(x, dp, k))
            return x

        last = far // 2
        mine_sa = far_gather(student_a, dp)
        mine_sa, x_other, teacher_a, teacher_b = tie(mine_sa, x_other, teacher_a, teacher_b)
        a_sa = near_a(mine_sa, dp)
        ta, tb = far_all(teacher_a), far_all(teacher_b)
        a_sa, ta, s_head = tie(a_sa, ta, s_head)
        both_sa = join(mine_sa, a_sa)
        b_sa = near_b(both_sa, dp)
        ta_in = far_step(ta, dp, last)
        b_sa, ta_in, tb = tie(b_sa, ta_in, tb)
        mine_ta = join(ta, ta_in)
        a_ta = near_a(mine_ta, dp)
        tb_in = far_step(tb, dp, last)
        pieces_sa = [both_sa, b_sa]
    else:

        def gathered(x, sizes):
            parts, at = [], 0
            for n in sizes:
                parts.append(lax.all_gather(x[at : at + n], "dp", axis=0, tiled=True))
                at += n
            return [jnp.concatenate(parts, axis=0)]

        a_rows, b_rows = 3 * HALF_D, 2 * HALF_F + HALF_D
        pieces_sa = gathered(student_a, (c, c, c))
        pieces_ta = gathered(teacher_a, (c, c, c))
        pieces_tb = gathered(teacher_b, (f, f, c))
        pieces_sb = gathered(student_b, (f, f, c))
        others_tb = [swap(p, dp) for p in pieces_tb]
        others_sb = [swap(p, dp) for p in pieces_sb]

    q, k, v, w_qkv = project(ids, tokens, x_other, s_head, pieces_sa, a_rows)
    if fast:
        q, a_ta, student_b = tie(q, a_ta, student_b)
        both_ta = join(mine_ta, a_ta)
        b_ta = near_b(both_ta, dp)
        sb = far_all(student_b)
    ctx_0, logs_0 = attend(0, 1, ids, q, k, v, True)
    if fast:
        ctx_0, q, tb_in, sb = tie(ctx_0, q, tb_in, sb)
        mine_tb = join(tb, tb_in)
        a_tb = near_a(mine_tb, dp)
        sb_in = far_step(sb, dp, last)
    ctx_1, logs_1 = attend(1, 2, ids, q, k, v, True)
    if fast:
        ctx_1, a_tb, b_ta = tie(ctx_1, a_tb, b_ta)
        pieces_ta = [both_ta, b_ta]
        both_tb = join(mine_tb, a_tb)
        b_tb = near_b(both_tb, dp)
        others_tb = [swap(both_tb, dp)]
    ctx = [ctx_0, ctx_1]
    ctx_other = swap(halves(ctx), dp)
    tq, tk, tv, _ = project(ids, tokens, x_other, t_head, pieces_ta, a_rows)
    if fast:
        tq, sb_in = tie(tq, sb_in)
        mine_sb = join(sb, sb_in)
        a_sb = near_a(mine_sb, dp)
    t_ctx_0 = attend(0, 2, ids, tq, tk, tv, False)[0]
    if fast:
        t_ctx_0, tq, b_tb, a_sb, ctx_other = tie(t_ctx_0, tq, b_tb, a_sb, ctx_other)
        pieces_tb = [both_tb, b_tb]
        others_tb.append(swap(b_tb, dp))
        both_sb = join(mine_sb, a_sb)
        b_sb = near_b(both_sb, dp)
        others_sb = [swap(both_sb, dp)]
    t_ctx = [t_ctx_0, attend(2, 1, ids, tq, tk, tv, False)[0]]
    t_other = swap(halves(t_ctx), dp)
    y = teacher_ffn(ids, tokens, t_ctx, t_other, t_row, t_unit, pieces_tb, others_tb, b_rows)
    if fast:
        y, b_sb = tie(y, b_sb)
        pieces_sb = [both_sb, b_sb]
        others_sb.append(swap(b_sb, dp))
    (student, act, gpre, hid, gffn, gbr, gmix, g_own, g_send, sums, unit_sums) = student_ffn(
        ids, tokens, ctx, ctx_other, y, s_row, s_unit, pieces_sb, others_sb, b_rows
    )
    g_other = swap(g_send, dp)

    away = ffn_grads(ids, act, gpre, [ctx_other], hid, gffn, gbr, b_rows, dp, fast, False)
    gpre, *away = tie(gpre, *away)
    away = [swap(p, dp) for p in away]
    home = ffn_grads(ids, act, gpre, ctx, hid, gffn, gbr, b_rows, dp, fast, True)

    ctx_all = jnp.concatenate(ctx, axis=2)
    logs = jnp.concatenate([logs_0, logs_1], axis=0)

    def back(at, n):
        return attend_back(at, n, ids, q, k, v, ctx_all, g_own, g_other, logs)

    def near_sum(own, other, received):
        n = own.shape[0] // 2
        terms = (own, *other, received)
        onward = plus(*[x[n:] for x in terms]).astype(BF)
        return [x[:n] for x in terms], near_a(onward, dp)

    if fast:
        away_b = plus(home[1], away[1]).astype(BF)
        g_other, away_b, away[0] = tie(g_other, away_b, away[0])
        b_in = near_b(away_b, dp)
        grads = list(back(0, 2))
        grads[0], k, b_in = tie(grads[0], k, b_in)
        kept, a_in = near_sum(home[0], [away[0]], b_in)
        grads += back(2, 1)
        grads[3], a_in = tie(grads[3], a_in)
        b_grad = direct_sum(plus(*kept, a_in), dp)
        up_grad, down_grad, out_grad = b_grad[:f], b_grad[f : 2 * f], b_grad[2 * f :]
    else:
        grads = list(back(0, 2)) + list(back(2, 1))
        up_grad, down_grad, out_grad = [
            lax.psum_scatter(a + b, "dp", scatter_dimension=0, tiled=True)
            for a, b in zip(home, away)
        ]

    a_pieces = qkv_grads(ids, grads, tokens, x_other, a_rows, dp, fast)
    if fast:
        grads[0], *a_pieces = tie(grads[0], *a_pieces)
        b_in = near_b(a_pieces[1], dp)
        b_in, *grads = tie(b_in, *grads)
        kept, a_in = near_sum(a_pieces[0], [], b_in)
        qkv_grad = direct_sum(plus(*kept, a_in), dp).reshape(3, c, D)
    else:
        qkv_grad = lax.psum_scatter(
            a_pieces[0].reshape(3, HALF_D, D), "dp", scatter_dimension=1, tiled=True
        )

    gq, gk, gv = [jnp.concatenate(grads[j::3], axis=1) for j in range(3)]
    back_rows = jnp.concatenate([gq, gk, gv], axis=1)
    theirs = lax.dynamic_slice_in_dim(back_rows, (1 - t) * HALF_L, HALF_L, 0)
    ours = lax.dynamic_slice_in_dim(back_rows, t * HALF_L, HALF_L, 0)
    back_other = swap(nn(theirs, w_qkv).astype(BF), dp)
    token_grad = gmix + nn(ours, w_qkv) + back_other.astype(F32)

    head_sums = jnp.stack(
        [jnp.sum(gq.astype(F32), axis=0), jnp.sum(gv.astype(F32), axis=0)]
    )
    head_sums = lax.dynamic_update_slice_in_dim(
        jnp.zeros((2, D), F32), head_sums, t * HALF_D, 1
    )
    small_grads = jnp.concatenate(
        [
            head_sums.reshape(2, n_dev, c).transpose(1, 0, 2).reshape(n_dev, 2 * c),
            unit_sums[0].reshape(n_dev, f),
            sums[:6].reshape(6, n_dev, c).transpose(1, 0, 2).reshape(n_dev, 6 * c),
        ],
        axis=1,
    )
    small_grads = jnp.sum(lax.all_to_all(small_grads, BOTH, 0, 0), axis=0)

    return (
        student,
        token_grad,
        jnp.transpose(qkv_grad, (0, 2, 1)),
        out_grad,
        jnp.transpose(up_grad),
        down_grad,
        small_grads[: 2 * c].reshape(2, c),
        small_grads[2 * c : 2 * c + f],
        small_grads[2 * c + f :].reshape(6, c),
    )


def solution(mesh):
    both, weight = ("dp", "tensor"), ("tensor", "dp")
    params_spec = (
        P(None, None, weight),
        P(weight, None),
        P(None, weight),
        P(weight, None),
        P(None, both),
        P(both),
        P(None, both),
    )
    return jax.shard_map(
        local,
        mesh=mesh,
        in_specs=(P(both, None), P("dp")) + params_spec + params_spec,
        out_specs=(P(both, None), P(both, None)) + params_spec,
        check_vma=False,
    )
```
